32 devices in a mesh: tm: 32 (over z, y, x, core).
Axes of the slice: x: 2, y: 2, z: 4, core: 2. Of those that a mesh axis runs over, the one named last changes fastest.
Arguments:
- samples: float32 [32, 2, 256, 256], P('tm'), may hold values from -0.5 to 0.5
Outputs:
- propagators: float32 [32, 2, 256, 256], P('tm')
The draws below stay inside these ranges and needn't reach their ends.
All inputs are finite; a program needn't handle non-finite values.
Results may differ from the reference program's by a relative error of at most 0.0003.
Values sent between devices are 32-bit elements; how exact they have to be, the bound alone decides.
No kernel may reach another device: no remote copies, remote signals or barrier semaphores. Data moves between devices by JAX's collectives and lax.ppermute only.
A program may use at most 64 MiB of HBM per device.

```python
import jax
import jax.numpy as jnp
from jax import lax

D = 256
SLICES = 32


def steps_of(key, extent, shards, low, largest):
    def one(position, shards_of):
        heights = jax.random.uniform(jax.random.fold_in(jax.random.fold_in(key, 6), position), (shards_of,), jnp.float32, low / len(shards), largest / len(shards))
        return jnp.repeat(jnp.exp(heights), extent[position] // shards_of).reshape((-1,) + (1,) * (len(extent) - position - 1))

    loudness = one(*shards[0])
    for cut in shards[1:]:
        loudness = loudness * one(*cut)
    return loudness


def centred(rng, shape, width, most, cuts=(), kind=jnp.bfloat16):
    array = width * jax.random.normal(rng, shape, jnp.float32)
    if cuts:
        array = array * steps_of(rng, shape, cuts, -0.22, 0.18)
    return jnp.clip(array, -most, most).astype(kind)


def setup_inputs(seed: int = 0) -> dict:
    seeds = jax.random.split(jax.random.key(seed), 2)
    samples = centred(seeds[0], (SLICES, 2, D, D), (4 * D // 9) ** -0.5, 0.5, ((0, 32),), jnp.float32)
    return {"samples": samples}


time_step = 0.25


def complex_product(left, right):
    size = left.shape[-1]
    joined = jnp.concatenate([right[0], right[1]], axis=1)
    real_rows = jnp.dot(left[0], joined, preferred_element_type=jnp.float32, precision=lax.Precision.HIGHEST)
    imag_rows = jnp.dot(left[1], joined, preferred_element_type=jnp.float32, precision=lax.Precision.HIGHEST)
    real_part = real_rows[:, :size] - imag_rows[:, size:]
    imag_part = real_rows[:, size:] + imag_rows[:, :size]
    return jnp.stack([real_part, imag_part])


def hermitian(drawn):
    return jnp.stack([(drawn[0] + drawn[0].T) * 0.5, (drawn[1] - drawn[1].T) * 0.5])


def unit_matrix(size):
    return jnp.stack([jnp.eye(size, dtype=jnp.float32), jnp.zeros((size, size), jnp.float32)])


def magnus_factor(first, second):
    size = first.shape[-1]
    summed = first + second
    product = complex_product(second, first)
    comm_real = product[0] - product[0].T
    comm_imag = product[1] + product[1].T
    shrink = time_step * time_step / 12.0
    omega = jnp.stack([0.5 * time_step * summed[1] - shrink * comm_real,
                       -0.5 * time_step * summed[0] - shrink * comm_imag])
    identity = unit_matrix(size)
    nested = identity + omega / 4.0
    nested = identity + complex_product(omega, nested) / 3.0
    nested = identity + complex_product(omega, nested) / 2.0
    return identity + complex_product(omega, nested)


def reference(samples):
    current = jax.vmap(hermitian)(samples)
    following = jnp.roll(current, -1, axis=0)
    factors = lax.map(lambda pair: magnus_factor(pair[0], pair[1]), (current, following))

    def advance(carry, factor):
        fresh = complex_product(factor, carry)
        return fresh, fresh

    start = unit_matrix(samples.shape[-1])
    _, cumulative = lax.scan(advance, start, factors)
    return cumulative
```

```python
import functools

import jax
import jax.numpy as jnp
from jax import lax
from jax.experimental import pallas as pl
from jax.experimental.pallas import tpu as pltpu
from jax.sharding import PartitionSpec as P


time_step = 0.25
plane = 8
parts = 8


def exchanged(x, axis, mask):
    size = lax.axis_size(axis)
    return lax.ppermute(x, axis, [(i, i ^ mask) for i in range(size)])


def from_next(x, axis):
    size = lax.axis_size(axis)
    return lax.ppermute(x, axis, [(i, (i - 1) % size) for i in range(size)])


def split(x):
    high = x.astype(jnp.bfloat16)
    low = (x - high.astype(jnp.float32)).astype(jnp.bfloat16)
    return high, low


def halves(pair):
    real, imag = split(pair[0]), split(pair[1])
    return (real[0], imag[0]), (real[1], imag[1])


def dot(left, right, turned):
    dims = (((1,), (1 if turned else 0,)), ((), ()))
    return lax.dot_general(left, right, dims, preferred_element_type=jnp.float32)


def product(left, right, turned=False):
    (lrh, lih), (lrl, lil) = left
    (rrh, rih), (rrl, ril) = right
    rows = lrh.shape[0]
    high = jnp.concatenate([lrh, lih], axis=0)
    low = jnp.concatenate([lrl, lil], axis=0)
    by_real = dot(high, rrh, turned) + (dot(high, rrl, turned) + dot(low, rrh, turned))
    by_imag = dot(high, rih, turned) + (dot(high, ril, turned) + dot(low, rih, turned))
    return by_real[:rows] - by_imag[rows:], by_imag[:rows] + by_real[rows:]


def call(kernel, outs, scratch, flops, *args):
    as_list = isinstance(outs, list)
    shapes = outs if as_list else [outs]
    moved = sum(a.size * a.dtype.itemsize for a in args)
    moved += sum(s.size * s.dtype.itemsize for s in shapes)
    vmem = pl.BlockSpec(memory_space=pltpu.VMEM)
    return pl.pallas_call(
        kernel,
        out_shape=outs,
        in_specs=[vmem] * len(args),
        out_specs=[vmem] * len(shapes) if as_list else vmem,
        scratch_shapes=scratch,
        compiler_params=pltpu.CompilerParams(vmem_limit_bytes=24 * 1024 * 1024),
        cost_estimate=pl.CostEstimate(flops=flops, bytes_accessed=moved, transcendentals=0),
    )(*args)


def f32(*shape):
    return jax.ShapeDtypeStruct(shape, jnp.float32)


def index_grid(size):
    row = lax.broadcasted_iota(jnp.int32, (size, size), 0)
    col = lax.broadcasted_iota(jnp.int32, (size, size), 1)
    return row, col


def pack_kernel(drawn_ref, packed_ref):
    first, second = drawn_ref[0, 0], drawn_ref[0, 1]
    row, col = index_grid(first.shape[0])
    mirrored = jnp.where(row >= col, first, -second).T
    packed_ref[...] = (jnp.where(row <= col, first, second) + mirrored) * 0.5


def unpacked(packed):
    row, col = index_grid(packed.shape[0])
    mirrored = packed.T
    real = jnp.where(row <= col, packed, mirrored)
    imag = jnp.where(row > col, packed, jnp.where(row < col, -mirrored, 0.0))
    return real, imag


def factor_kernel(first_ref, second_ref, factor_ref):
    first = unpacked(first_ref[...])
    second = unpacked(second_ref[...])
    row, col = index_grid(first[0].shape[0])
    identity = jnp.where(row == col, 1.0, 0.0).astype(jnp.float32)
    both = product(halves(second), halves(first))
    comm_real = both[0] - both[0].T
    comm_imag = both[1] + both[1].T
    shrink = time_step * time_step / 12.0
    real = 0.5 * time_step * (first[1] + second[1]) - shrink * comm_real
    imag = -0.5 * time_step * (first[0] + second[0]) - shrink * comm_imag
    real = -real
    exponent = halves((real, imag))
    nested = (identity + real * 0.25, imag * 0.25)
    for order in (3.0, 2.0, 1.0):
        grown = product(exponent, halves(nested))
        nested = (identity + grown[0] * (1.0 / order), grown[1] * (1.0 / order))
    factor_ref[0] = nested[0]
    factor_ref[1] = nested[1]


def load(ref, rows=slice(None)):
    return ref[0, rows, :], ref[1, rows, :]


def store(ref, pair, rows=slice(None)):
    ref[0, rows, :] = pair[0]
    ref[1, rows, :] = pair[1]


def chip_kernel(axis, own_ref, other_ref, half_ref):
    odd = lax.axis_index(axis) & 1
    rows = half_ref.shape[1]
    half = pl.ds(pl.multiple_of(odd * rows, rows), rows)

    @pl.when(odd == 0)
    def _():
        store(half_ref, product(halves(load(own_ref, half)), halves(load(other_ref))))

    @pl.when(odd == 1)
    def _():
        store(half_ref, product(halves(load(other_ref, half)), halves(load(own_ref))))


def get(high_ref, low_ref, q, rows=slice(None)):
    return (
        (high_ref[q, 0, rows, :], high_ref[q, 1, rows, :]),
        (low_ref[q, 0, rows, :], low_ref[q, 1, rows, :]),
    )


def picked(pair, chosen):
    high, low = pair
    return tuple(
        dot(chosen, high[k], True) + dot(chosen, low[k], True) for k in range(2)
    )


def one_hot_rows(count, size, begin):
    row = lax.broadcasted_iota(jnp.int32, (count, size), 0)
    col = lax.broadcasted_iota(jnp.int32, (count, size), 1)
    return jnp.where(row + begin == col, 1.0, 0.0).astype(jnp.bfloat16)


def gather_kernel(axis, level, *refs):
    in_refs, (slice_ref, high_ref, low_ref) = refs[:8], refs[8:]
    me = lax.axis_index(axis)
    odd, chip = me & 1, (me >> 1) & 3
    size = high_ref.shape[-1]
    half = size // 2
    for rel in range(4):
        for other in range(2):
            begin = pl.multiple_of((odd ^ other) * half, half)
            for k in range(2):
                high, low = split(in_refs[2 * rel + other][k])
                high_ref[chip ^ rel, k, pl.ds(begin, half), :] = high
                low_ref[chip ^ rel, k, pl.ds(begin, half), :] = low
    count = size // parts
    begin = pl.multiple_of((me & (parts - 1)) * count, count)
    upper = (me // level) & 1

    @pl.when(upper == 0)
    def _():
        value = get(high_ref, low_ref, 0, pl.ds(begin, count))
        for q in (1, 2, 3):
            grown = product(value, get(high_ref, low_ref, q))
            value = halves(grown)
        store(slice_ref, grown)

    @pl.when(upper == 1)
    def _():
        chosen = one_hot_rows(count, size, begin)
        grown = picked(get(high_ref, low_ref, 3), chosen)
        for q in (2, 1, 0):
            grown = product(halves(grown), get(high_ref, low_ref, q), True)
        store(slice_ref, grown)


def prefix_kernel(axis, high_ref, low_ref, own_ref, total_ref, local_ref):
    me = lax.axis_index(axis)
    odd, chip = me & 1, (me >> 1) & 3
    first = get(high_ref, low_ref, 0)

    @pl.when((chip == 0) & (odd == 1))
    def _():
        for k in range(2):
            local_ref[k] = first[0][k].astype(jnp.float32) + first[1][k].astype(jnp.float32)

    @pl.when((chip == 0) & (odd == 0))
    def _():
        store(local_ref, load(own_ref))

    value = first
    for q in (1, 2, 3):

        @pl.when((chip == q) & (odd == 0))
        def _(value=value):
            store(local_ref, product(value, halves(load(own_ref))))

        grown = product(value, get(high_ref, low_ref, q))
        store(total_ref, grown)
        value = halves(load(total_ref))

        @pl.when((chip == q) & (odd == 1))
        def _():
            store(local_ref, load(total_ref))


def cut_kernel(axis, level, total_ref, slice_ref):
    me = lax.axis_index(axis)
    count, size = slice_ref.shape[1], slice_ref.shape[2]
    begin = pl.multiple_of((me & (parts - 1)) * count, count)
    upper = (me // level) & 1

    @pl.when(upper == 0)
    def _():
        store(slice_ref, load(total_ref, pl.ds(begin, count)))

    @pl.when(upper == 1)
    def _():
        store(slice_ref, picked(halves(load(total_ref)), one_hot_rows(count, size, begin)))


def double_kernel(axis, level, total_ref, local_ref, mine_ref, other_ref, next_total_ref, next_local_ref):
    me = lax.axis_index(axis)
    odd, upper = me & 1, (me // level) & 1
    half = mine_ref.shape[1]
    top = [jnp.where(odd == 0, mine_ref[k], other_ref[k]) for k in range(2)]
    low = [jnp.where(odd == 0, other_ref[k], mine_ref[k]) for k in range(2)]
    came = halves([jnp.concatenate([top[k], low[k]], axis=0) for k in range(2)])
    total = halves(load(total_ref))

    @pl.when(upper == 0)
    def _():
        store(next_total_ref, product(total, came))
        store(next_local_ref, load(local_ref))

    @pl.when(upper == 1)
    def _():
        store(next_total_ref, product(came, total))
        store(next_local_ref, product(came, halves(load(local_ref))))


def step_kernel(axis, level, came_ref, total_ref, slice_ref):
    upper = (lax.axis_index(axis) // level) & 1
    came = halves(load(came_ref))
    total = halves(load(total_ref))

    @pl.when(upper == 0)
    def _():
        store(slice_ref, product(came, total, True))

    @pl.when(upper == 1)
    def _():
        store(slice_ref, product(came, total))


def assemble(axis, in_refs, whole_ref):
    me = lax.axis_index(axis) & (parts - 1)
    count = in_refs[0].shape[1]
    for k, ref in enumerate(in_refs):
        begin = pl.multiple_of((me ^ k) * count, count)
        store(whole_ref, load(ref), pl.ds(begin, count))


def local_kernel(axis, level, *refs):
    in_refs, local_ref, out_ref, whole_ref = refs[:8], refs[8], refs[9], refs[10]
    upper = (lax.axis_index(axis) // level) & 1

    @pl.when(upper == 0)
    def _():
        for k in range(2):
            out_ref[k] = local_ref[k].T

    @pl.when(upper == 1)
    def _():
        assemble(axis, in_refs, whole_ref)
        grown = product(halves(load(whole_ref)), halves(load(local_ref)))
        for k in range(2):
            out_ref[k] = grown[k].T


def final_kernel(axis, level, *refs):
    in_refs, local_ref, out_ref, whole_ref = refs[:8], refs[8], refs[9], refs[10]
    block = (lax.axis_index(axis) // level) & 3

    def put(pair):
        out_ref[0, 0] = pair[0]
        out_ref[0, 1] = pair[1]

    @pl.when(block < 2)
    def _():
        put(load(local_ref))

    @pl.when(block >= 2)
    def _():
        assemble(axis, in_refs, whole_ref)

    @pl.when(block == 2)
    def _():
        put(product(halves(load(local_ref)), halves(load(whole_ref))))

    @pl.when(block == 3)
    def _():
        put(product(halves(load(local_ref)), halves(load(whole_ref)), True))


def plane_slices(mine, axis):
    even = [mine] + [exchanged(mine, axis, mask) for mask in (2, 4, 6)]
    odd = [exchanged(piece, axis, 1) for piece in even]
    return [piece for both in zip(even, odd) for piece in both]


def on_device(samples):
    axis = "tm"
    devices = lax.axis_size(axis)
    size = samples.shape[-1]
    cube = 8 * size**3
    part = size // parts
    whole = f32(2, size, size)
    strip = f32(2, part, size)

    packed = call(pack_kernel, f32(size, size), [], size * size, samples)
    factor = call(factor_kernel, whole, [], 12 * cube, packed, from_next(packed, axis))
    other = exchanged(factor, axis, 1)
    half = call(
        functools.partial(chip_kernel, axis), f32(2, size // 2, size), [], 3 * cube // 2, factor, other
    )
    received = [half] + [exchanged(half, axis, mask) for mask in (2, 4, 6)]
    pieces = [p for piece in received for p in (piece, exchanged(piece, axis, 1))]

    level = plane
    split_shape = jax.ShapeDtypeStruct((4, 2, size, size), jnp.bfloat16)
    mine, high, low = call(
        functools.partial(gather_kernel, axis, level), [strip, split_shape, split_shape], [], cube, *pieces
    )
    total, local = call(
        functools.partial(prefix_kernel, axis), [whole, whole], [], 12 * cube, high, low, factor
    )
    if devices > 4 * plane:
        while 4 * level < devices:
            came = exchanged(lax.dynamic_slice_in_dim(total, (lax.axis_index(axis) & 1) * (size // 2), size // 2, 1), axis, level)
            paired = exchanged(came, axis, 1)
            total, local = call(
                functools.partial(double_kernel, axis, level), [whole, whole], [], 6 * cube, total, local, came, paired
            )
            level = 2 * level
        mine = call(functools.partial(cut_kernel, axis, level), strip, [], cube, total)
    came = exchanged(mine, axis, level)
    step = call(functools.partial(step_kernel, axis, level), strip, [], 3 * cube // parts, came, total)
    below = exchanged(step, axis, 2 * level)
    room = [pltpu.VMEM((2, size, size), jnp.float32)]
    local = call(
        functools.partial(local_kernel, axis, level), whole, room, 3 * cube, *plane_slices(came, axis), local
    )
    return call(
        functools.partial(final_kernel, axis, level),
        f32(1, 2, size, size),
        room,
        3 * cube,
        *plane_slices(below, axis),
        local,
    )


def solution(mesh):
    in_specs = (P("tm", None, None, None),)
    out_specs = P("tm", None, None, None)
    return jax.shard_map(
        on_device, mesh=mesh, in_specs=in_specs, out_specs=out_specs, check_vma=False
    )
```

```python
import functools

import jax
import jax.numpy as jnp
from jax import lax
from jax.experimental import pallas as pl
from jax.experimental.pallas import tpu as pltpu
from jax.sharding import PartitionSpec as P


time_step = 0.25
plane = 8
parts = 8


def exchanged(x, axis, mask):
    size = lax.axis_size(axis)
    return lax.ppermute(x, axis, [(i, i ^ mask) for i in range(size)])


def from_next(x, axis):
    size = lax.axis_size(axis)
    return lax.ppermute(x, axis, [(i, (i - 1) % size) for i in range(size)])


def split(x):
    high = x.astype(jnp.bfloat16)
    low = (x - high.astype(jnp.float32)).astype(jnp.bfloat16)
    return high, low


def halves(pair):
    real, imag = split(pair[0]), split(pair[1])
    return (real[0], imag[0]), (real[1], imag[1])


def dot(left, right, turned):
    dims = (((1,), (1 if turned else 0,)), ((), ()))
    return lax.dot_general(left, right, dims, preferred_element_type=jnp.float32)


def product(left, right, turned=False):
    (lrh, lih), (lrl, lil) = left
    (rrh, rih), (rrl, ril) = right
    rows = lrh.shape[0]
    high = jnp.concatenate([lrh, lih], axis=0)
    low = jnp.concatenate([lrl, lil], axis=0)
    by_real = dot(high, rrh, turned) + (dot(high, rrl, turned) + dot(low, rrh, turned))
    by_imag = dot(high, rih, turned) + (dot(high, ril, turned) + dot(low, rih, turned))
    return by_real[:rows] - by_imag[rows:], by_imag[:rows] + by_real[rows:]


def call(kernel, outs, scratch, flops, *args):
    as_list = isinstance(outs, list)
    shapes = outs if as_list else [outs]
    moved = sum(a.size * a.dtype.itemsize for a in args)
    moved += sum(s.size * s.dtype.itemsize for s in shapes)
    vmem = pl.BlockSpec(memory_space=pltpu.VMEM)
    return pl.pallas_call(
        kernel,
        out_shape=outs,
        in_specs=[vmem] * len(args),
        out_specs=[vmem] * len(shapes) if as_list else vmem,
        scratch_shapes=scratch,
        compiler_params=pltpu.CompilerParams(vmem_limit_bytes=24 * 1024 * 1024),
        cost_estimate=pl.CostEstimate(flops=flops, bytes_accessed=moved, transcendentals=0),
    )(*args)


def f32(*shape):
    return jax.ShapeDtypeStruct(shape, jnp.float32)


def index_grid(size):
    row = lax.broadcasted_iota(jnp.int32, (size, size), 0)
    col = lax.broadcasted_iota(jnp.int32, (size, size), 1)
    return row, col


def pack_kernel(drawn_ref, packed_ref):
    first, second = drawn_ref[0, 0], drawn_ref[0, 1]
    row, col = index_grid(first.shape[0])
    mirrored = jnp.where(row >= col, first, -second).T
    packed_ref[...] = (jnp.where(row <= col, first, second) + mirrored) * 0.5


def unpacked(packed):
    row, col = index_grid(packed.shape[0])
    mirrored = packed.T
    real = jnp.where(row <= col, packed, mirrored)
    imag = jnp.where(row > col, packed, jnp.where(row < col, -mirrored, 0.0))
    return real, imag


def factor_kernel(first_ref, second_ref, factor_ref):
    first = unpacked(first_ref[...])
    second = unpacked(second_ref[...])
    row, col = index_grid(first[0].shape[0])
    identity = jnp.where(row == col, 1.0, 0.0).astype(jnp.float32)
    both = product(halves(second), halves(first))
    comm_real = both[0] - both[0].T
    comm_imag = both[1] + both[1].T
    shrink = time_step * time_step / 12.0
    real = 0.5 * time_step * (first[1] + second[1]) - shrink * comm_real
    imag = -0.5 * time_step * (first[0] + second[0]) - shrink * comm_imag
    real = -real
    exponent = halves((real, imag))
    nested = (identity + real * 0.25, imag * 0.25)
    for order in (3.0, 2.0, 1.0):
        grown = product(exponent, halves(nested))
        nested = (identity + grown[0] * (1.0 / order), grown[1] * (1.0 / order))
    factor_ref[0] = nested[0]
    factor_ref[1] = nested[1]


def load(ref, rows=slice(None)):
    return ref[0, rows, :], ref[1, rows, :]


def store(ref, pair, rows=slice(None)):
    ref[0, rows, :] = pair[0]
    ref[1, rows, :] = pair[1]


def chip_kernel(axis, own_ref, other_ref, half_ref):
    odd = lax.axis_index(axis) & 1
    rows = half_ref.shape[1]
    half = pl.ds(pl.multiple_of(odd * rows, rows), rows)

    @pl.when(odd == 0)
    def _():
        store(half_ref, product(halves(load(own_ref, half)), halves(load(other_ref))))

    @pl.when(odd == 1)
    def _():
        store(half_ref, product(halves(load(other_ref, half)), halves(load(own_ref))))


def get(high_ref, low_ref, q, rows=slice(None)):
    return (
        (high_ref[q, 0, rows, :], high_ref[q, 1, rows, :]),
        (low_ref[q, 0, rows, :], low_ref[q, 1, rows, :]),
    )


def picked(pair, chosen):
    high, low = pair
    return tuple(
        dot(chosen, high[k], True) + dot(chosen, low[k], True) for k in range(2)
    )


def one_hot_rows(count, size, begin):
    row = lax.broadcasted_iota(jnp.int32, (count, size), 0)
    col = lax.broadcasted_iota(jnp.int32, (count, size), 1)
    return jnp.where(row + begin == col, 1.0, 0.0).astype(jnp.bfloat16)


def gather_kernel(axis, level, *refs):
    in_refs, (slice_ref, high_ref, low_ref) = refs[:8], refs[8:]
    me = lax.axis_index(axis)
    odd, chip = me & 1, (me >> 1) & 3
    size = high_ref.shape[-1]
    half = size // 2
    for rel in range(4):
        for other in range(2):
            begin = pl.multiple_of((odd ^ other) * half, half)
            for k in range(2):
                high, low = split(in_refs[2 * rel + other][k])
                high_ref[chip ^ rel, k, pl.ds(begin, half), :] = high
                low_ref[chip ^ rel, k, pl.ds(begin, half), :] = low
    count = size // parts
    begin = pl.multiple_of((me & (parts - 1)) * count, count)
    upper = (me // level) & 1

    @pl.when(upper == 0)
    def _():
        value = get(high_ref, low_ref, 0, pl.ds(begin, count))
        for q in (1, 2, 3):
            grown = product(value, get(high_ref, low_ref, q))
            value = halves(grown)
        store(slice_ref, grown)

    @pl.when(upper == 1)
    def _():
        chosen = one_hot_rows(count, size, begin)
        grown = picked(get(high_ref, low_ref, 3), chosen)
        for q in (2, 1, 0):
            grown = product(halves(grown), get(high_ref, low_ref, q), True)
        store(slice_ref, grown)


def prefix_kernel(axis, high_ref, low_ref, own_ref, total_ref, local_ref):
    me = lax.axis_index(axis)
    odd, chip = me & 1, (me >> 1) & 3
    first = get(high_ref, low_ref, 0)

    @pl.when((chip == 0) & (odd == 1))
    def _():
        for k in range(2):
            local_ref[k] = first[0][k].astype(jnp.float32) + first[1][k].astype(jnp.float32)

    @pl.when((chip == 0) & (odd == 0))
    def _():
        store(local_ref, load(own_ref))

    value = first
    for q in (1, 2, 3):

        @pl.when((chip == q) & (odd == 0))
        def _(value=value):
            store(local_ref, product(value, halves(load(own_ref))))

        grown = product(value, get(high_ref, low_ref, q))
        store(total_ref, grown)
        value = halves(load(total_ref))

        @pl.when((chip == q) & (odd == 1))
        def _():
            store(local_ref, load(total_ref))


def cut_kernel(axis, level, total_ref, slice_ref):
    me = lax.axis_index(axis)
    count, size = slice_ref.shape[1], slice_ref.shape[2]
    begin = pl.multiple_of((me & (parts - 1)) * count, count)
    upper = (me // level) & 1

    @pl.when(upper == 0)
    def _():
        store(slice_ref, load(total_ref, pl.ds(begin, count)))

    @pl.when(upper == 1)
    def _():
        store(slice_ref, picked(halves(load(total_ref)), one_hot_rows(count, size, begin)))


def double_kernel(axis, level, total_ref, local_ref, mine_ref, other_ref, next_total_ref, next_local_ref):
    me = lax.axis_index(axis)
    odd, upper = me & 1, (me // level) & 1
    top = [jnp.where(odd == 0, mine_ref[k], other_ref[k]) for k in range(2)]
    low = [jnp.where(odd == 0, other_ref[k], mine_ref[k]) for k in range(2)]
    came = halves([jnp.concatenate([top[k], low[k]], axis=0) for k in range(2)])
    total = halves(load(total_ref))

    @pl.when(upper == 0)
    def _():
        store(next_total_ref, product(total, came))
        store(next_local_ref, load(local_ref))

    @pl.when(upper == 1)
    def _():
        store(next_total_ref, product(came, total))
        store(next_local_ref, product(came, halves(load(local_ref))))


def step_kernel(axis, level, came_ref, total_ref, slice_ref):
    upper = (lax.axis_index(axis) // level) & 1
    came = halves(load(came_ref))
    total = halves(load(total_ref))

    @pl.when(upper == 0)
    def _():
        store(slice_ref, product(came, total, True))

    @pl.when(upper == 1)
    def _():
        store(slice_ref, product(came, total))


def assemble(axis, in_refs, whole_ref):
    me = lax.axis_index(axis) & (parts - 1)
    count = in_refs[0].shape[1]
    for k, ref in enumerate(in_refs):
        begin = pl.multiple_of((me ^ k) * count, count)
        store(whole_ref, load(ref), pl.ds(begin, count))


def local_kernel(axis, level, *refs):
    in_refs, local_ref, out_ref, whole_ref = refs[:8], refs[8], refs[9], refs[10]
    upper = (lax.axis_index(axis) // level) & 1

    @pl.when(upper == 0)
    def _():
        for k in range(2):
            out_ref[k] = local_ref[k].T

    @pl.when(upper == 1)
    def _():
        assemble(axis, in_refs, whole_ref)
        grown = product(halves(load(whole_ref)), halves(load(local_ref)))
        for k in range(2):
            out_ref[k] = grown[k].T


def final_kernel(axis, level, *refs):
    in_refs, local_ref, out_ref, whole_ref = refs[:8], refs[8], refs[9], refs[10]
    block = (lax.axis_index(axis) // level) & 3

    def put(pair):
        out_ref[0, 0] = pair[0]
        out_ref[0, 1] = pair[1]

    @pl.when(block < 2)
    def _():
        put(load(local_ref))

    @pl.when(block >= 2)
    def _():
        assemble(axis, in_refs, whole_ref)

    @pl.when(block == 2)
    def _():
        put(product(halves(load(local_ref)), halves(load(whole_ref))))

    @pl.when(block == 3)
    def _():
        put(product(halves(load(local_ref)), halves(load(whole_ref)), True))


def plane_slices(mine, axis):
    even = [mine] + [exchanged(mine, axis, mask) for mask in (2, 4, 6)]
    odd = [exchanged(piece, axis, 1) for piece in even]
    return [piece for both in zip(even, odd) for piece in both]


def cumulative(samples):
    axis = "tm"
    devices = lax.axis_size(axis)
    size = samples.shape[-1]
    cube = 8 * size**3
    part = size // parts
    whole = f32(2, size, size)
    strip = f32(2, part, size)

    packed = call(pack_kernel, f32(size, size), [], size * size, samples)
    factor = call(factor_kernel, whole, [], 12 * cube, packed, from_next(packed, axis))
    other = exchanged(factor, axis, 1)
    half = call(functools.partial(chip_kernel, axis), f32(2, size // 2, size), [], 3 * cube // 2, factor, other)
    received = [half] + [exchanged(half, axis, mask) for mask in (2, 4, 6)]
    pieces = [p for piece in received for p in (piece, exchanged(piece, axis, 1))]

    level = plane
    split_shape = jax.ShapeDtypeStruct((4, 2, size, size), jnp.bfloat16)
    mine, high, low = call(
        functools.partial(gather_kernel, axis, level), [strip, split_shape, split_shape], [], cube, *pieces
    )
    total, local = call(functools.partial(prefix_kernel, axis), [whole, whole], [], 12 * cube, high, low, factor)
    if devices > 4 * plane:
        while 4 * level < devices:
            half_of = lax.dynamic_slice_in_dim(total, (lax.axis_index(axis) & 1) * (size // 2), size // 2, 1)
            came = exchanged(half_of, axis, level)
            paired = exchanged(came, axis, 1)
            total, local = call(
                functools.partial(double_kernel, axis, level), [whole, whole], [], 6 * cube, total, local, came, paired
            )
            level = 2 * level
        mine = call(functools.partial(cut_kernel, axis, level), strip, [], cube, total)
    came = exchanged(mine, axis, level)
    step = call(functools.partial(step_kernel, axis, level), strip, [], 3 * cube // parts, came, total)
    below = exchanged(step, axis, 2 * level)
    room = [pltpu.VMEM((2, size, size), jnp.float32)]
    local = call(functools.partial(local_kernel, axis, level), whole, room, 3 * cube, *plane_slices(came, axis), local)
    return call(
        functools.partial(final_kernel, axis, level),
        f32(1, 2, size, size),
        room,
        3 * cube,
        *plane_slices(below, axis),
        local,
    )


def solution(mesh):
    in_specs = (P("tm", None, None, None),)
    out_specs = P("tm", None, None, None)
    return jax.shard_map(cumulative, mesh=mesh, in_specs=in_specs, out_specs=out_specs, check_vma=False)
```

```python
import functools

import jax
import jax.numpy as jnp
from jax import lax
from jax.experimental import pallas as pl
from jax.experimental.pallas import tpu as pltpu
from jax.sharding import PartitionSpec as P


time_step = 0.25
plane = 8
parts = 8


def exchanged(x, axis, mask):
    size = lax.axis_size(axis)
    return lax.ppermute(x, axis, [(i, i ^ mask) for i in range(size)])


def from_next(x, axis):
    size = lax.axis_size(axis)
    target = {i: i - 1 for i in range(1, size)}
    target[0] = size - plane
    target[size - plane + 1] = size - 1
    return lax.ppermute(x, axis, sorted(target.items()))


def to_last(x, axis):
    size = lax.axis_size(axis)
    return lax.ppermute(x, axis, [(size - plane, size - 1)])


def split(x):
    high = x.astype(jnp.bfloat16)
    low = (x - high.astype(jnp.float32)).astype(jnp.bfloat16)
    return high, low


def halves(pair):
    real, imag = split(pair[0]), split(pair[1])
    return (real[0], imag[0]), (real[1], imag[1])


def dot(left, right, turned):
    dims = (((1,), (1 if turned else 0,)), ((), ()))
    return lax.dot_general(left, right, dims, preferred_element_type=jnp.float32)


def product(left, right, turned=False):
    (lrh, lih), (lrl, lil) = left
    (rrh, rih), (rrl, ril) = right
    rows = lrh.shape[0]
    high = jnp.concatenate([lrh, lih], axis=0)
    low = jnp.concatenate([lrl, lil], axis=0)
    by_real = dot(high, rrh, turned) + (dot(high, rrl, turned) + dot(low, rrh, turned))
    by_imag = dot(high, rih, turned) + (dot(high, ril, turned) + dot(low, rih, turned))
    return by_real[:rows] - by_imag[rows:], by_imag[:rows] + by_real[rows:]


def call(kernel, outs, scratch, flops, *args, aliases={}):
    as_list = isinstance(outs, list)
    shapes = outs if as_list else [outs]
    moved = sum(a.size * a.dtype.itemsize for a in args)
    moved += sum(s.size * s.dtype.itemsize for s in shapes)
    vmem = pl.BlockSpec(memory_space=pltpu.VMEM)
    return pl.pallas_call(
        kernel,
        out_shape=outs,
        in_specs=[vmem] * len(args),
        out_specs=[vmem] * len(shapes) if as_list else vmem,
        scratch_shapes=scratch,
        input_output_aliases=aliases,
        compiler_params=pltpu.CompilerParams(vmem_limit_bytes=24 * 1024 * 1024),
        cost_estimate=pl.CostEstimate(flops=flops, bytes_accessed=moved, transcendentals=0),
    )(*args)


def f32(*shape):
    return jax.ShapeDtypeStruct(shape, jnp.float32)


def index_grid(size):
    row = lax.broadcasted_iota(jnp.int32, (size, size), 0)
    col = lax.broadcasted_iota(jnp.int32, (size, size), 1)
    return row, col


def pack_kernel(drawn_ref, packed_ref):
    first, second = drawn_ref[0, 0], drawn_ref[0, 1]
    row, col = index_grid(first.shape[0])
    mirrored = jnp.where(row >= col, first, -second).T
    packed_ref[...] = (jnp.where(row <= col, first, second) + mirrored) * 0.5


def unpacked(packed):
    row, col = index_grid(packed.shape[0])
    mirrored = packed.T
    real = jnp.where(row <= col, packed, mirrored)
    imag = jnp.where(row > col, packed, jnp.where(row < col, -mirrored, 0.0))
    return real, imag


def thirds(pair):
    return split(pair[0]), split(pair[1]), split(pair[0] + pair[1])


def three_products(left, right):
    def real(l, r):
        return dot(l[0], r[0], False) + (dot(l[0], r[1], False) + dot(l[1], r[0], False))

    ac, bd = real(left[0], right[0]), real(left[1], right[1])
    return ac - bd, real(left[2], right[2]) - (ac + bd)


def prepare_kernel(packed_ref, parts_ref, high_ref, low_ref):
    pair = unpacked(packed_ref[...])
    store(parts_ref, pair)
    for k, (high, low) in enumerate(thirds(pair)):
        high_ref[k] = high
        low_ref[k] = low


def magnus(parts_ref, high_ref, low_ref, packed, factor_ref):
    first = parts_ref[0], parts_ref[1]
    second = unpacked(packed)
    row, col = index_grid(packed.shape[0])
    identity = jnp.where(row == col, 1.0, 0.0).astype(jnp.float32)
    prepared = [(high_ref[k], low_ref[k]) for k in range(3)]
    both = three_products(thirds(second), prepared)
    comm_real = both[0] - both[0].T
    comm_imag = both[1] + both[1].T
    shrink = time_step * time_step / 12.0
    real = shrink * comm_real - 0.5 * time_step * (first[1] + second[1])
    imag = -0.5 * time_step * (first[0] + second[0]) - shrink * comm_imag
    exponent = thirds((real, imag))
    nested = (identity + real * 0.25, imag * 0.25)
    for order in (3.0, 2.0, 1.0):
        grown = three_products(thirds(nested), exponent)
        nested = (identity + grown[0] * (1.0 / order), grown[1] * (1.0 / order))
    factor_ref[0] = nested[0]
    factor_ref[1] = nested[1]


def factor_kernel(axis, parts_ref, high_ref, low_ref, pair_ref, next_ref, factor_ref):
    odd = lax.axis_index(axis) & 1
    magnus(parts_ref, high_ref, low_ref, jnp.where(odd == 0, pair_ref[...], next_ref[...]), factor_ref)


def late_kernel(axis, parts_ref, high_ref, low_ref, next_ref, factor_ref):
    me = lax.axis_index(axis)

    @pl.when(me == lax.axis_size(axis) - 1)
    def _():
        magnus(parts_ref, high_ref, low_ref, next_ref[...], factor_ref)


def load(ref, rows=slice(None)):
    return ref[0, rows, :], ref[1, rows, :]


def store(ref, pair, rows=slice(None)):
    ref[0, rows, :] = pair[0]
    ref[1, rows, :] = pair[1]


def chip_kernel(axis, own_ref, other_ref, half_ref, real_ref, imag_ref):
    odd = lax.axis_index(axis) & 1
    rows = half_ref.shape[1]
    half = pl.ds(pl.multiple_of(odd * rows, rows), rows)

    def put(left, right):
        pair = product(halves(left), halves(right))
        store(half_ref, pair)
        real_ref[...] = pair[0]
        imag_ref[...] = pair[1]

    @pl.when(odd == 0)
    def _():
        put(load(own_ref, half), load(other_ref))

    @pl.when(odd == 1)
    def _():
        put(load(other_ref, half), load(own_ref))


def get(high_ref, low_ref, q, rows=slice(None)):
    return (
        (high_ref[q, 0, rows, :], high_ref[q, 1, rows, :]),
        (low_ref[q, 0, rows, :], low_ref[q, 1, rows, :]),
    )


def get_pair(high_ref, low_ref, rows=slice(None)):
    return (
        (high_ref[0, rows, :], high_ref[1, rows, :]),
        (low_ref[0, rows, :], low_ref[1, rows, :]),
    )


def hold(axis, rel, other, k, piece, high_ref, low_ref):
    me = lax.axis_index(axis)
    rows = piece.shape[0]
    begin = pl.multiple_of(((me & 1) ^ other) * rows, rows)
    high, low = split(piece)
    high_ref[((me >> 1) & 3) ^ rel, k, pl.ds(begin, rows), :] = high
    low_ref[((me >> 1) & 3) ^ rel, k, pl.ds(begin, rows), :] = low


def near_kernel(axis, *refs):
    own, rest, (high_ref, low_ref, row_high_ref, row_low_ref) = refs[:2], refs[2:10], refs[10:]
    for k in range(2):
        for other in range(2):
            hold(axis, 0, other, k, own[other][k], high_ref, low_ref)
            hold(axis, 1, other, k, rest[2 * k + other][...], high_ref, low_ref)
            hold(axis, 2, other, k, rest[4 + 2 * k + other][...], high_ref, low_ref)
    begin = (lax.axis_index(axis) >> 1) & 2
    grown = product(get(high_ref, low_ref, begin), get(high_ref, low_ref, begin + 1))
    for k in range(2):
        row_high_ref[k], row_low_ref[k] = split(grown[k])


def core_rows(me, count):
    return pl.ds(pl.multiple_of((me & 1) * count, count), count)


def own_rows(me, count):
    return pl.ds(pl.multiple_of((me & (parts - 1)) * count, count), count)


def own_turned(me, count, columns, room_ref):
    begin = (me & (parts - 1)) * count
    width = room_ref.shape[0]
    block = pl.ds(pl.multiple_of(begin // width * width, width), width)
    inside = pl.ds(pl.multiple_of(begin % width, count), count)
    out = []
    for k in range(2):
        room_ref[...] = columns(k, block).T
        out.append(room_ref[inside, :])
    return out


def summed(high, low):
    return high.astype(jnp.float32) + low.astype(jnp.float32)


def total_kernel(axis, level, *refs):
    pieces, (row_high_ref, row_low_ref) = refs[:4], refs[6:8]
    slice_ref, high_ref, low_ref, room_ref = refs[8:]
    for k in range(2):
        for other in range(2):
            hold(axis, 3, other, k, pieces[2 * k + other][...], high_ref, low_ref)
    me = lax.axis_index(axis)
    rows = own_rows(me, slice_ref.shape[1])
    upper, second_row = (me // level) & 1, (me >> 2) & 1
    row = get_pair(row_high_ref, row_low_ref)

    @pl.when((upper == 0) & (second_row == 0))
    def _():
        value = product(get_pair(row_high_ref, row_low_ref, rows), get(high_ref, low_ref, 2))
        store(slice_ref, product(halves(value), get(high_ref, low_ref, 3)))

    @pl.when((upper == 0) & (second_row == 1))
    def _():
        value = product(get(high_ref, low_ref, 0, rows), get(high_ref, low_ref, 1))
        store(slice_ref, product(halves(value), row))

    @pl.when((upper == 1) & (second_row == 1))
    def _():
        value = own_turned(me, slice_ref.shape[1], lambda k, c: summed(row_high_ref[k, :, c], row_low_ref[k, :, c]), room_ref)
        value = product(halves(value), get(high_ref, low_ref, 1), True)
        store(slice_ref, product(halves(value), get(high_ref, low_ref, 0), True))

    @pl.when((upper == 1) & (second_row == 0))
    def _():
        value = own_turned(me, slice_ref.shape[1], lambda k, c: summed(high_ref[3, k, :, c], low_ref[3, k, :, c]), room_ref)
        value = product(halves(value), get(high_ref, low_ref, 2), True)
        store(slice_ref, product(halves(value), row, True))


def prefix_kernel(axis, high_ref, low_ref, own_ref, other_ref, total_ref, local_ref, half_ref):
    me = lax.axis_index(axis)
    odd, chip = me & 1, (me >> 1) & 3
    last = me == lax.axis_size(axis) - 1
    first = get(high_ref, low_ref, 0)

    @pl.when((chip == 0) & (odd == 1))
    def _():
        for k in range(2):
            local_ref[k] = first[0][k].astype(jnp.float32) + first[1][k].astype(jnp.float32)

    @pl.when((chip == 0) & (odd == 0))
    def _():
        store(local_ref, load(own_ref))

    value = first
    for q in (1, 2, 3):

        @pl.when((chip == q) & (odd == 0))
        def _(value=value):
            store(local_ref, product(value, halves(load(own_ref))))

        if q == 3:

            @pl.when(last)
            def _(value=value):
                store(local_ref, product(value, halves(load(other_ref))))

        grown = product(value, get(high_ref, low_ref, q))
        store(total_ref, grown)
        value = halves(load(total_ref))

        @pl.when((chip == q) & (odd == 1) & jnp.logical_not(last))
        def _():
            store(local_ref, load(total_ref))

    store(half_ref, load(total_ref, core_rows(me, half_ref.shape[1])))


def cut_kernel(axis, level, total_ref, slice_ref, half_ref, room_ref):
    me = lax.axis_index(axis)
    count = slice_ref.shape[1]
    upper = (me // level) & 1
    store(half_ref, load(total_ref, core_rows(me, half_ref.shape[1])))

    @pl.when(upper == 0)
    def _():
        store(slice_ref, load(total_ref, own_rows(me, count)))

    @pl.when(upper == 1)
    def _():
        store(slice_ref, own_turned(me, count, lambda k, c: total_ref[k, :, c], room_ref))


def double_kernel(axis, level, total_ref, local_ref, mine_ref, other_ref, next_total_ref, next_local_ref):
    me = lax.axis_index(axis)
    odd, upper = me & 1, (me // level) & 1
    top = [jnp.where(odd == 0, mine_ref[k], other_ref[k]) for k in range(2)]
    low = [jnp.where(odd == 0, other_ref[k], mine_ref[k]) for k in range(2)]
    came = halves([jnp.concatenate([top[k], low[k]], axis=0) for k in range(2)])
    total = halves(load(total_ref))

    @pl.when(upper == 0)
    def _():
        store(next_total_ref, product(total, came))
        store(next_local_ref, load(local_ref))

    @pl.when(upper == 1)
    def _():
        store(next_total_ref, product(came, total))
        store(next_local_ref, product(came, halves(load(local_ref))))


def step_kernel(axis, level, came_ref, total_ref, slice_ref):
    upper = (lax.axis_index(axis) // level) & 1
    came = halves(load(came_ref))
    total = halves(load(total_ref))

    @pl.when(upper == 0)
    def _():
        store(slice_ref, product(came, total, True))

    @pl.when(upper == 1)
    def _():
        store(slice_ref, product(came, total))


def assemble(axis, in_refs, whole_ref):
    me = lax.axis_index(axis) & (parts - 1)
    count = in_refs[0].shape[1]
    for k, ref in enumerate(in_refs):
        begin = pl.multiple_of((me ^ k) * count, count)
        store(whole_ref, load(ref), pl.ds(begin, count))


def local_kernel(axis, level, mine_ref, twin_ref, local_ref, late_ref, out_ref, whole_ref):
    me = lax.axis_index(axis)
    half = mine_ref.shape[1]
    upper = (me // level) & 1
    last = me == lax.axis_size(axis) - 1

    @pl.when(upper == 0)
    def _():
        for k in range(2):
            out_ref[k] = local_ref[k].T

    @pl.when(upper == 1)
    def _():
        store(whole_ref, load(mine_ref), core_rows(me, half))
        store(whole_ref, load(twin_ref), core_rows(me ^ 1, half))
        store(whole_ref, product(halves(load(whole_ref)), halves(load(local_ref))))

    @pl.when(last)
    def _():
        store(whole_ref, product(halves(load(whole_ref)), halves(load(late_ref))))

    @pl.when(upper == 1)
    def _():
        for k in range(2):
            out_ref[k] = whole_ref[k].T


def final_kernel(axis, level, *refs):
    in_refs, local_ref, out_ref, whole_ref = refs[:8], refs[8], refs[9], refs[10]
    block = (lax.axis_index(axis) // level) & 3

    def put(pair):
        out_ref[0, 0] = pair[0]
        out_ref[0, 1] = pair[1]

    @pl.when(block < 2)
    def _():
        put(load(local_ref))

    @pl.when(block >= 2)
    def _():
        assemble(axis, in_refs, whole_ref)

    @pl.when(block == 2)
    def _():
        put(product(halves(load(local_ref)), halves(load(whole_ref))))

    @pl.when(block == 3)
    def _():
        put(product(halves(load(local_ref)), halves(load(whole_ref)), True))


def plane_slices(mine, axis):
    even = [mine] + [exchanged(mine, axis, mask) for mask in (2, 4, 6)]
    odd = [exchanged(piece, axis, 1) for piece in even]
    return [piece for both in zip(even, odd) for piece in both]


def cumulative(samples):
    axis = "tm"
    devices = lax.axis_size(axis)
    size = samples.shape[-1]
    cube = 8 * size**3
    part = size // parts
    whole = f32(2, size, size)
    strip = f32(2, part, size)

    packed = call(pack_kernel, f32(size, size), [], size * size, samples)
    near_next = from_next(packed, axis)
    even_next = exchanged(packed, axis, 1)
    last_next = to_last(near_next, axis)
    third_shape = jax.ShapeDtypeStruct((3, size, size), jnp.bfloat16)
    prepared = call(prepare_kernel, [whole, third_shape, third_shape], [], size * size, packed)
    factor = call(functools.partial(factor_kernel, axis), whole, [], 9 * cube, *prepared, even_next, near_next)
    other = exchanged(factor, axis, 1)
    quarter = f32(size // 2, size)
    half, real, imag = call(
        functools.partial(chip_kernel, axis),
        [f32(2, size // 2, size), quarter, quarter],
        [],
        3 * cube // 2,
        factor,
        other,
    )

    y_real = exchanged(real, axis, 4)
    x_imag = exchanged(imag, axis, 2)
    y_imag = exchanged(imag, axis, 4)
    x_real = exchanged(real, axis, 2)
    far_real = exchanged(y_real, axis, 2)
    far_imag = exchanged(x_imag, axis, 4)
    both = [half, exchanged(half, axis, 1)]
    for piece in (x_real, x_imag, y_real, y_imag):
        both += [piece, exchanged(piece, axis, 1)]
    far = []
    for piece in (far_real, far_imag):
        far += [piece, exchanged(piece, axis, 1)]

    level = plane
    split_shape = jax.ShapeDtypeStruct((4, 2, size, size), jnp.bfloat16)
    row_shape = jax.ShapeDtypeStruct((2, size, size), jnp.bfloat16)
    high, low, row_high, row_low = call(
        functools.partial(near_kernel, axis), [split_shape, split_shape, row_shape, row_shape], [], 3 * cube, *both
    )
    turning = [pltpu.VMEM((128, size), jnp.float32)]
    mine, high, low = call(
        functools.partial(total_kernel, axis, level),
        [strip, split_shape, split_shape],
        turning,
        cube,
        *far,
        high,
        low,
        row_high,
        row_low,
        aliases={4: 1, 5: 2},
    )
    half_shape = f32(2, size // 2, size)
    total, local, bulk = call(
        functools.partial(prefix_kernel, axis), [whole, whole, half_shape], [], 12 * cube, high, low, factor, other
    )
    if devices > 4 * plane:
        while 4 * level < devices:
            half_of = lax.dynamic_slice_in_dim(total, (lax.axis_index(axis) & 1) * (size // 2), size // 2, 1)
            came = exchanged(half_of, axis, level)
            paired = exchanged(came, axis, 1)
            total, local = call(
                functools.partial(double_kernel, axis, level), [whole, whole], [], 6 * cube, total, local, came, paired
            )
            level = 2 * level
        mine, bulk = call(functools.partial(cut_kernel, axis, level), [strip, half_shape], turning, cube, total)
    came = exchanged(mine, axis, level)
    step = call(functools.partial(step_kernel, axis, level), strip, [], 3 * cube // parts, came, total)
    below = exchanged(step, axis, 2 * level)
    came_bulk = exchanged(bulk, axis, level)
    twin_bulk = exchanged(came_bulk, axis, 1)
    room = [pltpu.VMEM((2, size, size), jnp.float32)]
    late = call(functools.partial(late_kernel, axis), whole, [], cube, *prepared, last_next)
    local = call(functools.partial(local_kernel, axis, level), whole, room, 3 * cube, came_bulk, twin_bulk, local, late)
    return call(
        functools.partial(final_kernel, axis, level),
        f32(1, 2, size, size),
        room,
        3 * cube,
        *plane_slices(below, axis),
        local,
    )


def solution(mesh):
    in_specs = (P("tm", None, None, None),)
    out_specs = P("tm", None, None, None)
    return jax.shard_map(cumulative, mesh=mesh, in_specs=in_specs, out_specs=out_specs, check_vma=False)
```

```python
import functools

import jax
import jax.numpy as jnp
from jax import lax
from jax.experimental import pallas as pl
from jax.experimental.pallas import tpu as pltpu
from jax.sharding import PartitionSpec as P


time_step = 0.25
plane = 8
parts = 8


def exchanged(x, axis, mask):
    size = lax.axis_size(axis)
    return lax.ppermute(x, axis, [(i, i ^ mask) for i in range(size)])


def lower_exchanged(x, axis, level):
    size = lax.axis_size(axis)
    return lax.ppermute(x, axis, [(i, i ^ (level if (i // level) & 2 == 0 else 1)) for i in range(size)])


def upper_exchanged(x, axis, level, mask):
    size = lax.axis_size(axis)
    return lax.ppermute(x, axis, [(i, i ^ (mask if (i // level) & 2 else 1)) for i in range(size)])


def from_next(x, axis):
    size = lax.axis_size(axis)
    target = {i: i - 1 for i in range(1, size)}
    target[0] = size - plane
    target[size - plane + 1] = size - 1
    return lax.ppermute(x, axis, sorted(target.items()))


def to_last(x, axis):
    size = lax.axis_size(axis)
    return lax.ppermute(x, axis, [(size - plane, size - 1)])


def split(x):
    high = x.astype(jnp.bfloat16)
    low = (x - high.astype(jnp.float32)).astype(jnp.bfloat16)
    return high, low


def halves(pair):
    real, imag = split(pair[0]), split(pair[1])
    return (real[0], imag[0]), (real[1], imag[1])


def dot(left, right, turned):
    dims = (((1,), (1 if turned else 0,)), ((), ()))
    return lax.dot_general(left, right, dims, preferred_element_type=jnp.float32)


def product(left, right, turned=False):
    (lrh, lih), (lrl, lil) = left
    (rrh, rih), (rrl, ril) = right
    rows = lrh.shape[0]
    high = jnp.concatenate([lrh, lih], axis=0)
    low = jnp.concatenate([lrl, lil], axis=0)
    by_real = dot(high, rrh, turned) + (dot(high, rrl, turned) + dot(low, rrh, turned))
    by_imag = dot(high, rih, turned) + (dot(high, ril, turned) + dot(low, rih, turned))
    return by_real[:rows] - by_imag[rows:], by_imag[:rows] + by_real[rows:]


def call(kernel, outs, scratch, flops, *args, aliases={}, places=None, out_places=None):
    shapes = outs if isinstance(outs, list) else [outs]
    moved = sum(a.size * a.dtype.itemsize for a in args)
    moved += sum(s.size * s.dtype.itemsize for s in shapes)
    in_specs = [pl.BlockSpec(memory_space=p) for p in places or (pltpu.VMEM,) * len(args)]
    out_specs = [pl.BlockSpec(memory_space=p) for p in out_places or (pltpu.VMEM,) * len(shapes)]
    return pl.pallas_call(
        kernel,
        out_shape=outs,
        in_specs=in_specs,
        out_specs=out_specs if isinstance(outs, list) else out_specs[0],
        scratch_shapes=scratch,
        input_output_aliases=aliases,
        compiler_params=pltpu.CompilerParams(vmem_limit_bytes=24 * 1024 * 1024),
        cost_estimate=pl.CostEstimate(flops=flops, bytes_accessed=moved, transcendentals=0),
    )(*args)


def f32(*shape):
    return jax.ShapeDtypeStruct(shape, jnp.float32)


def index_grid(size):
    row = lax.broadcasted_iota(jnp.int32, (size, size), 0)
    col = lax.broadcasted_iota(jnp.int32, (size, size), 1)
    return row, col


def pack_kernel(drawn_ref, packed_ref):
    first, second = drawn_ref[0, 0], drawn_ref[0, 1]
    row, col = index_grid(first.shape[0])
    mirrored = jnp.where(row >= col, first, -second).T
    packed_ref[...] = (jnp.where(row <= col, first, second) + mirrored) * 0.5


def unpacked(packed):
    row, col = index_grid(packed.shape[0])
    mirrored = packed.T
    real = jnp.where(row <= col, packed, mirrored)
    imag = jnp.where(row > col, packed, jnp.where(row < col, -mirrored, 0.0))
    return real, imag


def thirds(pair):
    return split(pair[0]), split(pair[1]), split(pair[0] + pair[1])


def three_products(left, right):
    def real(l, r):
        return dot(l[0], r[0], False) + (dot(l[0], r[1], False) + dot(l[1], r[0], False))

    ac, bd = real(left[0], right[0]), real(left[1], right[1])
    return ac - bd, real(left[2], right[2]) - (ac + bd)


def prepare_kernel(packed_ref, parts_ref, high_ref, low_ref):
    pair = unpacked(packed_ref[...])
    store(parts_ref, pair)
    for k, (high, low) in enumerate(thirds(pair)):
        high_ref[k] = high
        low_ref[k] = low


def magnus(parts_ref, high_ref, low_ref, packed, factor_ref):
    first = parts_ref[0], parts_ref[1]
    second = unpacked(packed)
    row, col = index_grid(packed.shape[0])
    identity = jnp.where(row == col, 1.0, 0.0).astype(jnp.float32)
    prepared = [(high_ref[k], low_ref[k]) for k in range(3)]
    both = three_products(thirds(second), prepared)
    comm_real = both[0] - both[0].T
    comm_imag = both[1] + both[1].T
    shrink = time_step * time_step / 12.0
    real = shrink * comm_real - 0.5 * time_step * (first[1] + second[1])
    imag = -0.5 * time_step * (first[0] + second[0]) - shrink * comm_imag
    exponent = thirds((real, imag))
    nested = (identity + real * 0.25, imag * 0.25)
    for order in (3.0, 2.0, 1.0):
        grown = three_products(thirds(nested), exponent)
        nested = (identity + grown[0] * (1.0 / order), grown[1] * (1.0 / order))
    factor_ref[0] = nested[0]
    factor_ref[1] = nested[1]


def factor_kernel(axis, parts_ref, high_ref, low_ref, pair_ref, next_ref, factor_ref):
    odd = lax.axis_index(axis) & 1
    magnus(parts_ref, high_ref, low_ref, jnp.where(odd == 0, pair_ref[...], next_ref[...]), factor_ref)


def late_kernel(axis, parts_ref, high_ref, low_ref, next_ref, factor_ref):
    me = lax.axis_index(axis)

    @pl.when(me == lax.axis_size(axis) - 1)
    def _():
        magnus(parts_ref, high_ref, low_ref, next_ref[...], factor_ref)


def load(ref, rows=slice(None)):
    return ref[0, rows, :], ref[1, rows, :]


def store(ref, pair, rows=slice(None)):
    ref[0, rows, :] = pair[0]
    ref[1, rows, :] = pair[1]


def chip_kernel(axis, own_ref, other_ref, half_ref, real_ref, imag_ref):
    odd = lax.axis_index(axis) & 1
    rows = half_ref.shape[1]
    half = pl.ds(pl.multiple_of(odd * rows, rows), rows)

    def put(left, right):
        pair = product(halves(left), halves(right))
        store(half_ref, pair)
        real_ref[...] = pair[0]
        imag_ref[...] = pair[1]

    @pl.when(odd == 0)
    def _():
        put(load(own_ref, half), load(other_ref))

    @pl.when(odd == 1)
    def _():
        put(load(other_ref, half), load(own_ref))


def get(high_ref, low_ref, q, rows=slice(None)):
    return (
        (high_ref[q, 0, rows, :], high_ref[q, 1, rows, :]),
        (low_ref[q, 0, rows, :], low_ref[q, 1, rows, :]),
    )


def get_pair(high_ref, low_ref, rows=slice(None)):
    return (
        (high_ref[0, rows, :], high_ref[1, rows, :]),
        (low_ref[0, rows, :], low_ref[1, rows, :]),
    )


def hold(axis, rel, other, k, piece, high_ref, low_ref):
    me = lax.axis_index(axis)
    rows = piece.shape[0]
    begin = pl.multiple_of(((me & 1) ^ other) * rows, rows)
    high, low = split(piece)
    high_ref[((me >> 1) & 3) ^ rel, k, pl.ds(begin, rows), :] = high
    low_ref[((me >> 1) & 3) ^ rel, k, pl.ds(begin, rows), :] = low


def near_kernel(axis, *refs):
    own, rest, (high_ref, low_ref, row_high_ref, row_low_ref) = refs[:2], refs[2:10], refs[10:]
    for k in range(2):
        for other in range(2):
            hold(axis, 0, other, k, own[other][k], high_ref, low_ref)
            hold(axis, 1, other, k, rest[2 * k + other][...], high_ref, low_ref)
            hold(axis, 2, other, k, rest[4 + 2 * k + other][...], high_ref, low_ref)
    begin = (lax.axis_index(axis) >> 1) & 2
    grown = product(get(high_ref, low_ref, begin), get(high_ref, low_ref, begin + 1))
    for k in range(2):
        row_high_ref[k], row_low_ref[k] = split(grown[k])


def core_rows(me, count):
    return pl.ds(pl.multiple_of((me & 1) * count, count), count)


def own_rows(me, count):
    return pl.ds(pl.multiple_of((me & (parts - 1)) * count, count), count)


def own_turned(me, count, columns, room_ref):
    begin = (me & (parts - 1)) * count
    width = room_ref.shape[0]
    block = pl.ds(pl.multiple_of(begin // width * width, width), width)
    inside = pl.ds(pl.multiple_of(begin % width, count), count)
    out = []
    for k in range(2):
        room_ref[...] = columns(k, block).T
        out.append(room_ref[inside, :])
    return out


def summed(high, low):
    return high.astype(jnp.float32) + low.astype(jnp.float32)


def total_kernel(axis, level, *refs):
    pieces, (row_high_ref, row_low_ref) = refs[:4], refs[6:8]
    slice_ref, high_ref, low_ref, room_ref = refs[8:]
    for k in range(2):
        for other in range(2):
            hold(axis, 3, other, k, pieces[2 * k + other][...], high_ref, low_ref)
    me = lax.axis_index(axis)
    rows = own_rows(me, slice_ref.shape[1])
    upper, second_row = (me // level) & 1, (me >> 2) & 1
    row = get_pair(row_high_ref, row_low_ref)

    @pl.when((upper == 0) & (second_row == 0))
    def _():
        value = product(get_pair(row_high_ref, row_low_ref, rows), get(high_ref, low_ref, 2))
        store(slice_ref, product(halves(value), get(high_ref, low_ref, 3)))

    @pl.when((upper == 0) & (second_row == 1))
    def _():
        value = product(get(high_ref, low_ref, 0, rows), get(high_ref, low_ref, 1))
        store(slice_ref, product(halves(value), row))

    @pl.when((upper == 1) & (second_row == 1))
    def _():
        value = own_turned(me, slice_ref.shape[1], lambda k, c: summed(row_high_ref[k, :, c], row_low_ref[k, :, c]), room_ref)
        value = product(halves(value), get(high_ref, low_ref, 1), True)
        store(slice_ref, product(halves(value), get(high_ref, low_ref, 0), True))

    @pl.when((upper == 1) & (second_row == 0))
    def _():
        value = own_turned(me, slice_ref.shape[1], lambda k, c: summed(high_ref[3, k, :, c], low_ref[3, k, :, c]), room_ref)
        value = product(halves(value), get(high_ref, low_ref, 2), True)
        store(slice_ref, product(halves(value), row, True))


def prefix_kernel(axis, high_ref, low_ref, own_ref, other_ref, total_ref, local_ref, half_ref):
    me = lax.axis_index(axis)
    odd, chip = me & 1, (me >> 1) & 3
    last = me == lax.axis_size(axis) - 1
    first = get(high_ref, low_ref, 0)

    @pl.when((chip == 0) & (odd == 1))
    def _():
        for k in range(2):
            local_ref[k] = first[0][k].astype(jnp.float32) + first[1][k].astype(jnp.float32)

    @pl.when((chip == 0) & (odd == 0))
    def _():
        store(local_ref, load(own_ref))

    value = first
    for q in (1, 2, 3):

        @pl.when((chip == q) & (odd == 0))
        def _(value=value):
            store(local_ref, product(value, halves(load(own_ref))))

        if q == 3:

            @pl.when(last)
            def _(value=value):
                store(local_ref, product(value, halves(load(other_ref))))

        grown = product(value, get(high_ref, low_ref, q))
        store(total_ref, grown)
        value = halves(load(total_ref))

        @pl.when((chip == q) & (odd == 1) & jnp.logical_not(last))
        def _():
            store(local_ref, load(total_ref))

    store(half_ref, load(total_ref, core_rows(me, half_ref.shape[1])))


def cut_kernel(axis, level, total_ref, slice_ref, half_ref, room_ref):
    me = lax.axis_index(axis)
    count = slice_ref.shape[1]
    upper = (me // level) & 1
    store(half_ref, load(total_ref, core_rows(me, half_ref.shape[1])))

    @pl.when(upper == 0)
    def _():
        store(slice_ref, load(total_ref, own_rows(me, count)))

    @pl.when(upper == 1)
    def _():
        store(slice_ref, own_turned(me, count, lambda k, c: total_ref[k, :, c], room_ref))


def double_kernel(axis, level, total_ref, local_ref, mine_ref, other_ref, next_total_ref, next_local_ref):
    me = lax.axis_index(axis)
    odd, upper = me & 1, (me // level) & 1
    top = [jnp.where(odd == 0, mine_ref[k], other_ref[k]) for k in range(2)]
    low = [jnp.where(odd == 0, other_ref[k], mine_ref[k]) for k in range(2)]
    came = halves([jnp.concatenate([top[k], low[k]], axis=0) for k in range(2)])
    total = halves(load(total_ref))

    @pl.when(upper == 0)
    def _():
        store(next_total_ref, product(total, came))
        store(next_local_ref, load(local_ref))

    @pl.when(upper == 1)
    def _():
        store(next_total_ref, product(came, total))
        store(next_local_ref, product(came, halves(load(local_ref))))


def step_kernel(axis, level, came_ref, total_ref, slice_ref):
    upper = (lax.axis_index(axis) // level) & 1
    came = halves(load(came_ref))
    total = halves(load(total_ref))

    @pl.when(upper == 0)
    def _():
        store(slice_ref, product(came, total, True))

    @pl.when(upper == 1)
    def _():
        store(slice_ref, product(came, total))


def join_kernel(*refs):
    for place, ref in enumerate(refs[:4]):
        refs[4][place] = ref[...]


def assemble(axis, mine_ref, twin_ref, whole_ref):
    me = lax.axis_index(axis)
    for other, ref in enumerate((mine_ref, twin_ref)):
        for place in range(4):
            rows = own_rows(me ^ (2 * place + other), ref.shape[2])
            store(whole_ref, (ref[place, 0], ref[place, 1]), rows)


def local_kernel(axis, level, mine_ref, twin_ref, local_ref, late_ref, out_ref, high_ref, low_ref, whole_ref, sent):
    me = lax.axis_index(axis)
    half = mine_ref.shape[1]
    upper = (me // level) & 1
    block = (me // level) & 3
    last = me == lax.axis_size(axis) - 1

    @pl.when(upper == 0)
    def _():
        store(whole_ref, [local_ref[k].T for k in range(2)])

    @pl.when(upper == 1)
    def _():
        store(whole_ref, load(mine_ref), core_rows(me, half))
        store(whole_ref, load(twin_ref), core_rows(me ^ 1, half))
        grown = three_products(thirds(load(whole_ref)), thirds(load(local_ref)))

        @pl.when(jnp.logical_not(last))
        def _():
            store(whole_ref, [grown[k].T for k in range(2)])

        @pl.when(last)
        def _():
            ended = three_products(thirds(grown), thirds(load(late_ref)))
            store(whole_ref, [ended[k].T for k in range(2)])

    @pl.when(block < 2)
    def _():
        copy = pltpu.make_async_copy(whole_ref, out_ref.at[0], sent)
        copy.start()
        copy.wait()

    @pl.when(block >= 2)
    def _():
        for k, (high, low) in enumerate(thirds(load(whole_ref))):
            high_ref[k] = high
            low_ref[k] = low


def final_kernel(axis, level, mine_ref, twin_ref, high_ref, low_ref, done_ref, out_ref, whole_ref, result_ref, sent):
    block = (lax.axis_index(axis) // level) & 3
    steps = sent.shape[0]
    count = whole_ref.shape[1] // steps

    def put(turned):
        assemble(axis, mine_ref, twin_ref, whole_ref)
        whole = load(whole_ref)
        right = thirds([part.T for part in whole] if turned else whole)
        copies = []
        for step in range(steps):
            rows = pl.ds(step * count, count)
            left = [(high_ref[k, rows, :], low_ref[k, rows, :]) for k in range(3)]
            store(result_ref, three_products(left, right), rows)
            copies.append(
                pltpu.make_async_copy(result_ref.at[:, rows], out_ref.at[0, :, rows], sent.at[step])
            )
            copies[-1].start()
        for copy in copies:
            copy.wait()

    @pl.when(block == 2)
    def _():
        put(False)

    @pl.when(block == 3)
    def _():
        put(True)


def plane_slices(mine, axis, level):
    even = [mine] + [upper_exchanged(mine, axis, level, mask) for mask in (2, 4, 6)]
    shape = jax.ShapeDtypeStruct((4,) + mine.shape, mine.dtype)
    joined = call(join_kernel, shape, [], mine.size, *even)
    return joined, exchanged(joined, axis, 1)


def cumulative(samples):
    axis = "tm"
    devices = lax.axis_size(axis)
    size = samples.shape[-1]
    cube = 8 * size**3
    part = size // parts
    whole = f32(2, size, size)
    strip = f32(2, part, size)

    packed = call(pack_kernel, f32(size, size), [], size * size, samples)
    near_next = from_next(packed, axis)
    even_next = exchanged(packed, axis, 1)
    last_next = to_last(near_next, axis)
    third_shape = jax.ShapeDtypeStruct((3, size, size), jnp.bfloat16)
    prepared = call(prepare_kernel, [whole, third_shape, third_shape], [], size * size, packed)
    factor = call(functools.partial(factor_kernel, axis), whole, [], 9 * cube, *prepared, even_next, near_next)
    other = exchanged(factor, axis, 1)
    quarter = f32(size // 2, size)
    half, real, imag = call(
        functools.partial(chip_kernel, axis),
        [f32(2, size // 2, size), quarter, quarter],
        [],
        3 * cube // 2,
        factor,
        other,
    )

    y_real = exchanged(real, axis, 4)
    x_imag = exchanged(imag, axis, 2)
    y_imag = exchanged(imag, axis, 4)
    x_real = exchanged(real, axis, 2)
    far_real = exchanged(y_real, axis, 2)
    far_imag = exchanged(x_imag, axis, 4)
    both = [half, exchanged(half, axis, 1)]
    for piece in (x_real, x_imag, y_real, y_imag):
        both += [piece, exchanged(piece, axis, 1)]
    far = []
    for piece in (far_real, far_imag):
        far += [piece, exchanged(piece, axis, 1)]

    level = plane
    split_shape = jax.ShapeDtypeStruct((4, 2, size, size), jnp.bfloat16)
    row_shape = jax.ShapeDtypeStruct((2, size, size), jnp.bfloat16)
    high, low, row_high, row_low = call(
        functools.partial(near_kernel, axis), [split_shape, split_shape, row_shape, row_shape], [], 3 * cube, *both
    )
    turning = [pltpu.VMEM((128, size), jnp.float32)]
    mine, high, low = call(
        functools.partial(total_kernel, axis, level),
        [strip, split_shape, split_shape],
        turning,
        cube,
        *far,
        high,
        low,
        row_high,
        row_low,
        aliases={4: 1, 5: 2},
    )
    half_shape = f32(2, size // 2, size)
    total, local, bulk = call(
        functools.partial(prefix_kernel, axis), [whole, whole, half_shape], [], 12 * cube, high, low, factor, other
    )
    if devices > 4 * plane:
        while 4 * level < devices:
            half_of = lax.dynamic_slice_in_dim(total, (lax.axis_index(axis) & 1) * (size // 2), size // 2, 1)
            came = exchanged(half_of, axis, level)
            paired = exchanged(came, axis, 1)
            total, local = call(
                functools.partial(double_kernel, axis, level), [whole, whole], [], 6 * cube, total, local, came, paired
            )
            level = 2 * level
        mine, bulk = call(functools.partial(cut_kernel, axis, level), [strip, half_shape], turning, cube, total)
    came = lower_exchanged(mine, axis, level)
    step = call(functools.partial(step_kernel, axis, level), strip, [], 3 * cube // parts, came, total)
    below = exchanged(step, axis, 2 * level)
    came_bulk = exchanged(bulk, axis, level)
    twin_bulk = exchanged(came_bulk, axis, 1)
    room = [pltpu.VMEM((2, size, size), jnp.float32)]
    late = call(functools.partial(late_kernel, axis), whole, [], cube, *prepared, last_next)
    out_shape = f32(1, 2, size, size)
    out, high, low = call(
        functools.partial(local_kernel, axis, level),
        [out_shape, third_shape, third_shape],
        room + [pltpu.SemaphoreType.DMA(())],
        3 * cube,
        came_bulk,
        twin_bulk,
        local,
        late,
        out_places=(pl.ANY, pltpu.VMEM, pltpu.VMEM),
    )
    return call(
        functools.partial(final_kernel, axis, level),
        out_shape,
        room + room + [pltpu.SemaphoreType.DMA((2,))],
        3 * cube,
        *plane_slices(below, axis, level),
        high,
        low,
        out,
        places=(pltpu.VMEM,) * 4 + (pl.ANY,),
        out_places=(pl.ANY,),
        aliases={4: 0},
    )


def solution(mesh):
    in_specs = (P("tm", None, None, None),)
    out_specs = P("tm", None, None, None)
    return jax.shard_map(cumulative, mesh=mesh, in_specs=in_specs, out_specs=out_specs, check_vma=False)
```

```python
import functools

import jax
import jax.numpy as jnp
from jax import lax
from jax.experimental import pallas as pl
from jax.experimental.pallas import tpu as pltpu
from jax.sharding import PartitionSpec as P


time_step = 0.25
plane = 8
parts = 8


def exchanged(x, axis, mask):
    size = lax.axis_size(axis)
    return lax.ppermute(x, axis, [(i, i ^ mask) for i in range(size)])


def lower_exchanged(x, axis, level):
    size = lax.axis_size(axis)
    return lax.ppermute(x, axis, [(i, i ^ (level if (i // level) & 2 == 0 else 1)) for i in range(size)])


def upper_exchanged(x, axis, level, mask):
    size = lax.axis_size(axis)
    return lax.ppermute(x, axis, [(i, i ^ (mask if (i // level) & 2 else 1)) for i in range(size)])


def from_next(x, axis):
    size = lax.axis_size(axis)
    target = {i: i - 1 for i in range(1, size)}
    target[0] = size - plane
    target[size - plane + 1] = size - 1
    return lax.ppermute(x, axis, sorted(target.items()))


def to_last(x, axis):
    size = lax.axis_size(axis)
    return lax.ppermute(x, axis, [(size - plane, size - 1)])


def split(x):
    high = x.astype(jnp.bfloat16)
    low = (x - high.astype(jnp.float32)).astype(jnp.bfloat16)
    return high, low


def halves(pair):
    real, imag = split(pair[0]), split(pair[1])
    return (real[0], imag[0]), (real[1], imag[1])


def dot(left, right, turned):
    dims = (((1,), (1 if turned else 0,)), ((), ()))
    return lax.dot_general(left, right, dims, preferred_element_type=jnp.float32)


def product(left, right, turned=False):
    (lrh, lih), (lrl, lil) = left
    (rrh, rih), (rrl, ril) = right
    rows = lrh.shape[0]
    high = jnp.concatenate([lrh, lih], axis=0)
    low = jnp.concatenate([lrl, lil], axis=0)
    by_real = dot(high, rrh, turned) + (dot(high, rrl, turned) + dot(low, rrh, turned))
    by_imag = dot(high, rih, turned) + (dot(high, ril, turned) + dot(low, rih, turned))
    return by_real[:rows] - by_imag[rows:], by_imag[:rows] + by_real[rows:]


def columns_product(left, right):
    high, low = right
    width = high.shape[1] // 2

    def real(k):
        by_high = dot(left[0][k], high, False) + dot(left[1][k], high, False)
        return by_high + dot(left[0][k], low, False)

    by_real, by_imag = real(0), real(1)
    return by_real[:, :width] - by_imag[:, width:], by_real[:, width:] + by_imag[:, :width]


def call(kernel, outs, scratch, flops, *args, aliases={}, places=None, out_places=None):
    shapes = outs if isinstance(outs, list) else [outs]
    moved = sum(a.size * a.dtype.itemsize for a in args)
    moved += sum(s.size * s.dtype.itemsize for s in shapes)
    in_specs = [pl.BlockSpec(memory_space=p) for p in places or (pltpu.VMEM,) * len(args)]
    out_specs = [pl.BlockSpec(memory_space=p) for p in out_places or (pltpu.VMEM,) * len(shapes)]
    return pl.pallas_call(
        kernel,
        out_shape=outs,
        in_specs=in_specs,
        out_specs=out_specs if isinstance(outs, list) else out_specs[0],
        scratch_shapes=scratch,
        input_output_aliases=aliases,
        compiler_params=pltpu.CompilerParams(vmem_limit_bytes=24 * 1024 * 1024),
        cost_estimate=pl.CostEstimate(flops=flops, bytes_accessed=moved, transcendentals=0),
    )(*args)


def f32(*shape):
    return jax.ShapeDtypeStruct(shape, jnp.float32)


def index_grid(size):
    row = lax.broadcasted_iota(jnp.int32, (size, size), 0)
    col = lax.broadcasted_iota(jnp.int32, (size, size), 1)
    return row, col


def pack_kernel(drawn_ref, packed_ref):
    first, second = drawn_ref[0, 0], drawn_ref[0, 1]
    row, col = index_grid(first.shape[0])
    mirrored = jnp.where(row >= col, first, -second).T
    packed_ref[...] = (jnp.where(row <= col, first, second) + mirrored) * 0.5


def unpacked(packed):
    row, col = index_grid(packed.shape[0])
    mirrored = packed.T
    real = jnp.where(row <= col, packed, mirrored)
    imag = jnp.where(row > col, packed, jnp.where(row < col, -mirrored, 0.0))
    return real, imag


def thirds(pair):
    return split(pair[0]), split(pair[1]), split(pair[0] + pair[1])


def three_products(left, right):
    def real(l, r):
        return dot(l[0], r[0], False) + (dot(l[0], r[1], False) + dot(l[1], r[0], False))

    ac, bd = real(left[0], right[0]), real(left[1], right[1])
    return ac - bd, real(left[2], right[2]) - (ac + bd)


def prepare_kernel(packed_ref, parts_ref, high_ref, low_ref):
    pair = unpacked(packed_ref[...])
    store(parts_ref, pair)
    for k, (high, low) in enumerate(thirds(pair)):
        high_ref[k] = high
        low_ref[k] = low


def magnus(parts_ref, high_ref, low_ref, packed, factor_ref):
    first = parts_ref[0], parts_ref[1]
    second = unpacked(packed)
    row, col = index_grid(packed.shape[0])
    identity = jnp.where(row == col, 1.0, 0.0).astype(jnp.float32)
    prepared = [(high_ref[k], low_ref[k]) for k in range(3)]
    both = three_products(thirds(second), prepared)
    comm_real = both[0] - both[0].T
    comm_imag = both[1] + both[1].T
    shrink = time_step * time_step / 12.0
    real = shrink * comm_real - 0.5 * time_step * (first[1] + second[1])
    imag = -0.5 * time_step * (first[0] + second[0]) - shrink * comm_imag
    exponent = thirds((real, imag))
    nested = (identity + real * 0.25, imag * 0.25)
    for order in (3.0, 2.0, 1.0):
        grown = three_products(thirds(nested), exponent)
        nested = (identity + grown[0] * (1.0 / order), grown[1] * (1.0 / order))
    factor_ref[0] = nested[0]
    factor_ref[1] = nested[1]


def factor_kernel(axis, parts_ref, high_ref, low_ref, pair_ref, next_ref, factor_ref):
    odd = lax.axis_index(axis) & 1
    magnus(parts_ref, high_ref, low_ref, jnp.where(odd == 0, pair_ref[...], next_ref[...]), factor_ref)


def late_kernel(axis, parts_ref, high_ref, low_ref, next_ref, factor_ref):
    me = lax.axis_index(axis)

    @pl.when(me == lax.axis_size(axis) - 1)
    def _():
        magnus(parts_ref, high_ref, low_ref, next_ref[...], factor_ref)


def load(ref, rows=slice(None)):
    return ref[0, rows, :], ref[1, rows, :]


def store(ref, pair, rows=slice(None)):
    ref[0, rows, :] = pair[0]
    ref[1, rows, :] = pair[1]


def chip_kernel(axis, own_ref, other_ref, half_ref, real_ref, imag_ref):
    odd = lax.axis_index(axis) & 1
    rows = half_ref.shape[1]
    half = pl.ds(pl.multiple_of(odd * rows, rows), rows)

    def put(left, right):
        pair = product(halves(left), halves(right))
        store(half_ref, pair)
        real_ref[...] = pair[0]
        imag_ref[...] = pair[1]

    @pl.when(odd == 0)
    def _():
        put(load(own_ref, half), load(other_ref))

    @pl.when(odd == 1)
    def _():
        put(load(other_ref, half), load(own_ref))


def get(high_ref, low_ref, q, rows=slice(None)):
    return (
        (high_ref[q, 0, rows, :], high_ref[q, 1, rows, :]),
        (low_ref[q, 0, rows, :], low_ref[q, 1, rows, :]),
    )


def get_pair(high_ref, low_ref, rows=slice(None)):
    return (
        (high_ref[0, rows, :], high_ref[1, rows, :]),
        (low_ref[0, rows, :], low_ref[1, rows, :]),
    )


def hold(axis, rel, other, k, piece, high_ref, low_ref):
    me = lax.axis_index(axis)
    rows = piece.shape[0]
    begin = pl.multiple_of(((me & 1) ^ other) * rows, rows)
    high, low = split(piece)
    high_ref[((me >> 1) & 3) ^ rel, k, pl.ds(begin, rows), :] = high
    low_ref[((me >> 1) & 3) ^ rel, k, pl.ds(begin, rows), :] = low


def near_kernel(axis, *refs):
    own, rest, (high_ref, low_ref, row_high_ref, row_low_ref) = refs[:2], refs[2:10], refs[10:]
    for k in range(2):
        for other in range(2):
            hold(axis, 0, other, k, own[other][k], high_ref, low_ref)
            hold(axis, 1, other, k, rest[2 * k + other][...], high_ref, low_ref)
            hold(axis, 2, other, k, rest[4 + 2 * k + other][...], high_ref, low_ref)
    begin = (lax.axis_index(axis) >> 1) & 2
    grown = product(get(high_ref, low_ref, begin), get(high_ref, low_ref, begin + 1))
    for k in range(2):
        row_high_ref[k], row_low_ref[k] = split(grown[k])


def core_rows(me, count):
    return pl.ds(pl.multiple_of((me & 1) * count, count), count)


def own_rows(me, count):
    return pl.ds(pl.multiple_of((me & (parts - 1)) * count, count), count)


def own_turned(me, count, columns, room_ref):
    begin = (me & (parts - 1)) * count
    width = room_ref.shape[0]
    block = pl.ds(pl.multiple_of(begin // width * width, width), width)
    inside = pl.ds(pl.multiple_of(begin % width, count), count)
    out = []
    for k in range(2):
        room_ref[...] = columns(k, block).T
        out.append(room_ref[inside, :])
    return out


def total_kernel(axis, level, *refs):
    pieces, (row_high_ref, row_low_ref) = refs[:4], refs[6:8]
    slice_ref, high_ref, low_ref, room_ref = refs[8:]
    for k in range(2):
        for other in range(2):
            hold(axis, 3, other, k, pieces[2 * k + other][...], high_ref, low_ref)
    me = lax.axis_index(axis)
    rows = own_rows(me, slice_ref.shape[1])
    upper, second_row = (me // level) & 1, (me >> 2) & 1
    row = get_pair(row_high_ref, row_low_ref)

    @pl.when((upper == 0) & (second_row == 0))
    def _():
        value = product(get_pair(row_high_ref, row_low_ref, rows), get(high_ref, low_ref, 2))
        store(slice_ref, product(halves(value), get(high_ref, low_ref, 3)))

    @pl.when((upper == 0) & (second_row == 1))
    def _():
        value = product(get(high_ref, low_ref, 0, rows), get(high_ref, low_ref, 1))
        store(slice_ref, product(halves(value), row))

    begin = (me & (parts - 1)) * slice_ref.shape[1]
    width = room_ref.shape[0]
    block = pl.ds(pl.multiple_of(begin // width * width, width), width)

    def columns(high, low):
        return (
            jnp.concatenate([high[0], high[1]], axis=1),
            jnp.concatenate([low[0], low[1]], axis=1),
        )

    def put(first, second, right):
        grown = columns_product(first, right)
        grown = columns_product(second, columns(*zip(split(grown[0]), split(grown[1]))))
        inside = pl.ds(pl.multiple_of(begin % width, slice_ref.shape[1]), slice_ref.shape[1])
        for k in range(2):
            room_ref[...] = grown[k].T
            slice_ref[k] = room_ref[inside, :]

    @pl.when((upper == 1) & (second_row == 1))
    def _():
        right = columns(
            [row_high_ref[k, :, block] for k in range(2)], [row_low_ref[k, :, block] for k in range(2)]
        )
        put(get(high_ref, low_ref, 1), get(high_ref, low_ref, 0), right)

    @pl.when((upper == 1) & (second_row == 0))
    def _():
        right = columns(
            [high_ref[3, k, :, block] for k in range(2)], [low_ref[3, k, :, block] for k in range(2)]
        )
        put(get(high_ref, low_ref, 2), row, right)


def prefix_kernel(axis, high_ref, low_ref, own_ref, other_ref, total_ref, local_ref, half_ref):
    me = lax.axis_index(axis)
    odd, chip = me & 1, (me >> 1) & 3
    last = me == lax.axis_size(axis) - 1
    first = get(high_ref, low_ref, 0)

    @pl.when((chip == 0) & (odd == 1))
    def _():
        for k in range(2):
            local_ref[k] = first[0][k].astype(jnp.float32) + first[1][k].astype(jnp.float32)

    @pl.when((chip == 0) & (odd == 0))
    def _():
        store(local_ref, load(own_ref))

    value = first
    for q in (1, 2, 3):

        @pl.when((chip == q) & (odd == 0))
        def _(value=value):
            store(local_ref, product(value, halves(load(own_ref))))

        if q == 3:

            @pl.when(last)
            def _(value=value):
                store(local_ref, product(value, halves(load(other_ref))))

        grown = product(value, get(high_ref, low_ref, q))
        store(total_ref, grown)
        value = halves(load(total_ref))

        @pl.when((chip == q) & (odd == 1) & jnp.logical_not(last))
        def _():
            store(local_ref, load(total_ref))

    store(half_ref, load(total_ref, core_rows(me, half_ref.shape[1])))


def cut_kernel(axis, level, total_ref, slice_ref, half_ref, room_ref):
    me = lax.axis_index(axis)
    count = slice_ref.shape[1]
    upper = (me // level) & 1
    store(half_ref, load(total_ref, core_rows(me, half_ref.shape[1])))

    @pl.when(upper == 0)
    def _():
        store(slice_ref, load(total_ref, own_rows(me, count)))

    @pl.when(upper == 1)
    def _():
        store(slice_ref, own_turned(me, count, lambda k, c: total_ref[k, :, c], room_ref))


def double_kernel(axis, level, total_ref, local_ref, mine_ref, other_ref, next_total_ref, next_local_ref):
    me = lax.axis_index(axis)
    odd, upper = me & 1, (me // level) & 1
    top = [jnp.where(odd == 0, mine_ref[k], other_ref[k]) for k in range(2)]
    low = [jnp.where(odd == 0, other_ref[k], mine_ref[k]) for k in range(2)]
    came = halves([jnp.concatenate([top[k], low[k]], axis=0) for k in range(2)])
    total = halves(load(total_ref))

    @pl.when(upper == 0)
    def _():
        store(next_total_ref, product(total, came))
        store(next_local_ref, load(local_ref))

    @pl.when(upper == 1)
    def _():
        store(next_total_ref, product(came, total))
        store(next_local_ref, product(came, halves(load(local_ref))))


def step_kernel(axis, level, came_ref, total_ref, slice_ref):
    upper = (lax.axis_index(axis) // level) & 1
    came = halves(load(came_ref))
    total = halves(load(total_ref))

    @pl.when(upper == 0)
    def _():
        store(slice_ref, product(came, total, True))

    @pl.when(upper == 1)
    def _():
        store(slice_ref, product(came, total))


def join_kernel(*refs):
    for place, ref in enumerate(refs[:4]):
        refs[4][place] = ref[...]


def local_kernel(axis, level, mine_ref, twin_ref, local_ref, late_ref, out_ref, high_ref, low_ref, whole_ref, sent):
    me = lax.axis_index(axis)
    half, size = mine_ref.shape[1], local_ref.shape[-1]
    upper = (me // level) & 1
    block = (me // level) & 3
    last = me == lax.axis_size(axis) - 1

    def give(pair):
        for k, (high, low) in enumerate(thirds(pair)):
            high_ref[k] = high
            low_ref[k] = low

    def finish(pair):
        store(whole_ref, [part.T for part in pair])
        copy = pltpu.make_async_copy(whole_ref, out_ref.at[0], sent)
        copy.start()
        copy.wait()

    @pl.when(block == 0)
    def _():
        finish(load(local_ref))

    @pl.when(block == 2)
    def _():
        order = [own_rows(me ^ mask, size // parts) for mask in (0, 2, 4, 6, 1, 3, 5, 7)]
        give([jnp.concatenate([local_ref[k, rows, :] for rows in order], axis=0).T for k in range(2)])

    @pl.when(upper == 1)
    def _():
        store(whole_ref, load(mine_ref), core_rows(me, half))
        store(whole_ref, load(twin_ref), core_rows(me ^ 1, half))
        grown = three_products(thirds(load(whole_ref)), thirds(load(local_ref)))

        @pl.when(block == 1)
        def _():
            finish(grown)

        @pl.when((block == 3) & jnp.logical_not(last))
        def _():
            give(grown)

        @pl.when(last)
        def _():
            give(three_products(thirds(grown), thirds(load(late_ref))))


def joined_pair(ref):
    return [ref[:, k].reshape(-1, ref.shape[-1]) for k in range(2)]


def early_kernel(axis, level, mine_ref, high_ref, low_ref, part_ref):
    block = (lax.axis_index(axis) // level) & 3
    half = part_ref.shape[1] // 2

    @pl.when(block == 2)
    def _():
        left = [(high_ref[k, :, :half], low_ref[k, :, :half]) for k in range(3)]
        store(part_ref, three_products(left, thirds(joined_pair(mine_ref))))

    @pl.when(block == 3)
    def _():
        right = [(high_ref[k], low_ref[k]) for k in range(3)]
        store(part_ref, three_products(thirds(joined_pair(mine_ref)), right), pl.ds(0, half))


def final_kernel(axis, level, part_ref, twin_ref, high_ref, low_ref, done_ref, out_ref, whole_ref, result_ref, sent):
    me = lax.axis_index(axis)
    block = (me // level) & 3
    size = whole_ref.shape[1]
    half = size // 2
    spans = [pl.ds(0, half), pl.ds(half, half)]

    def send(step):
        copy = pltpu.make_async_copy(result_ref.at[:, spans[step]], out_ref.at[0, :, spans[step]], sent.at[step])
        copy.start()
        return copy

    @pl.when(block == 2)
    def _():
        right = thirds(joined_pair(twin_ref))
        copies = []
        for step, rows in enumerate(spans):
            left = [(high_ref[k, rows, half:], low_ref[k, rows, half:]) for k in range(3)]
            grown = three_products(left, right)
            store(result_ref, [part_ref[k, rows, :] + grown[k] for k in range(2)], rows)
            copies.append(send(step))
        for copy in copies:
            copy.wait()

    @pl.when(block == 3)
    def _():
        right = [(high_ref[k], low_ref[k]) for k in range(3)]
        grown = three_products(thirds(joined_pair(twin_ref)), right)
        count = size // parts
        for place in range(4):
            rows = slice(place * count, (place + 1) * count)
            store(whole_ref, load(part_ref, rows), own_rows(me ^ (2 * place), count))
            store(whole_ref, [part[rows] for part in grown], own_rows(me ^ (2 * place + 1), count))
        copies = []
        for step, columns in enumerate(spans):
            store(result_ref, [whole_ref[k, :, columns].T for k in range(2)], columns)
            copies.append(send(step))
        for copy in copies:
            copy.wait()


def plane_slices(mine, axis, level):
    even = [mine] + [upper_exchanged(mine, axis, level, mask) for mask in (2, 4, 6)]
    shape = jax.ShapeDtypeStruct((4,) + mine.shape, mine.dtype)
    joined = call(join_kernel, shape, [], mine.size, *even)
    return joined, exchanged(joined, axis, 1)


def cumulative(samples):
    axis = "tm"
    devices = lax.axis_size(axis)
    size = samples.shape[-1]
    cube = 8 * size**3
    part = size // parts
    whole = f32(2, size, size)
    strip = f32(2, part, size)

    packed = call(pack_kernel, f32(size, size), [], size * size, samples)
    near_next = from_next(packed, axis)
    even_next = exchanged(packed, axis, 1)
    last_next = to_last(near_next, axis)
    third_shape = jax.ShapeDtypeStruct((3, size, size), jnp.bfloat16)
    prepared = call(prepare_kernel, [whole, third_shape, third_shape], [], size * size, packed)
    factor = call(functools.partial(factor_kernel, axis), whole, [], 9 * cube, *prepared, even_next, near_next)
    other = exchanged(factor, axis, 1)
    quarter = f32(size // 2, size)
    half, real, imag = call(
        functools.partial(chip_kernel, axis),
        [f32(2, size // 2, size), quarter, quarter],
        [],
        3 * cube // 2,
        factor,
        other,
    )

    y_real = exchanged(real, axis, 4)
    x_imag = exchanged(imag, axis, 2)
    y_imag = exchanged(imag, axis, 4)
    x_real = exchanged(real, axis, 2)
    far_real = exchanged(y_real, axis, 2)
    far_imag = exchanged(x_imag, axis, 4)
    both = [half, exchanged(half, axis, 1)]
    for piece in (x_real, x_imag, y_real, y_imag):
        both += [piece, exchanged(piece, axis, 1)]
    far = []
    for piece in (far_real, far_imag):
        far += [piece, exchanged(piece, axis, 1)]

    level = plane
    split_shape = jax.ShapeDtypeStruct((4, 2, size, size), jnp.bfloat16)
    row_shape = jax.ShapeDtypeStruct((2, size, size), jnp.bfloat16)
    high, low, row_high, row_low = call(
        functools.partial(near_kernel, axis), [split_shape, split_shape, row_shape, row_shape], [], 3 * cube, *both
    )
    turning = [pltpu.VMEM((128, size), jnp.float32)]
    mine, high, low = call(
        functools.partial(total_kernel, axis, level),
        [strip, split_shape, split_shape],
        turning,
        cube,
        *far,
        high,
        low,
        row_high,
        row_low,
        aliases={4: 1, 5: 2},
    )
    half_shape = f32(2, size // 2, size)
    total, local, bulk = call(
        functools.partial(prefix_kernel, axis), [whole, whole, half_shape], [], 12 * cube, high, low, factor, other
    )
    if devices > 4 * plane:
        while 4 * level < devices:
            half_of = lax.dynamic_slice_in_dim(total, (lax.axis_index(axis) & 1) * (size // 2), size // 2, 1)
            came = exchanged(half_of, axis, level)
            paired = exchanged(came, axis, 1)
            total, local = call(
                functools.partial(double_kernel, axis, level), [whole, whole], [], 6 * cube, total, local, came, paired
            )
            level = 2 * level
        mine, bulk = call(functools.partial(cut_kernel, axis, level), [strip, half_shape], turning, cube, total)
    came = lower_exchanged(mine, axis, level)
    step = call(functools.partial(step_kernel, axis, level), strip, [], 3 * cube // parts, came, total)
    below = exchanged(step, axis, 2 * level)
    came_bulk = exchanged(bulk, axis, level)
    twin_bulk = exchanged(came_bulk, axis, 1)
    room = [pltpu.VMEM((2, size, size), jnp.float32)]
    late = call(functools.partial(late_kernel, axis), whole, [], cube, *prepared, last_next)
    out_shape = f32(1, 2, size, size)
    out, high, low = call(
        functools.partial(local_kernel, axis, level),
        [out_shape, third_shape, third_shape],
        room + [pltpu.SemaphoreType.DMA(())],
        3 * cube,
        came_bulk,
        twin_bulk,
        local,
        late,
        out_places=(pl.ANY, pltpu.VMEM, pltpu.VMEM),
    )
    joined, twin = plane_slices(below, axis, level)
    early = call(functools.partial(early_kernel, axis, level), whole, [], cube, joined, high, low)
    return call(
        functools.partial(final_kernel, axis, level),
        out_shape,
        room + room + [pltpu.SemaphoreType.DMA((2,))],
        2 * cube,
        early,
        twin,
        high,
        low,
        out,
        places=(pltpu.VMEM,) * 4 + (pl.ANY,),
        out_places=(pl.ANY,),
        aliases={4: 0},
    )


def solution(mesh):
    in_specs = (P("tm", None, None, None),)
    out_specs = P("tm", None, None, None)
    return jax.shard_map(cumulative, mesh=mesh, in_specs=in_specs, out_specs=out_specs, check_vma=False)
```

```python
import functools

import jax
import jax.numpy as jnp
from jax import lax
from jax.experimental import pallas as pl
from jax.experimental.pallas import tpu as pltpu
from jax.sharding import PartitionSpec as P


time_step = 0.25
plane = 8
parts = 8


def exchanged(x, axis, mask):
    size = lax.axis_size(axis)
    return lax.ppermute(x, axis, [(i, i ^ mask) for i in range(size)])


def lower_exchanged(x, axis, level):
    size = lax.axis_size(axis)
    return lax.ppermute(x, axis, [(i, i ^ (level if (i // level) & 2 == 0 else 1)) for i in range(size)])


def upper_exchanged(x, axis, level, mask):
    size = lax.axis_size(axis)
    return lax.ppermute(x, axis, [(i, i ^ (mask if (i // level) & 2 else 1)) for i in range(size)])


def from_next(x, axis):
    size = lax.axis_size(axis)
    target = {i: i - 1 for i in range(1, size)}
    target[0] = size - plane
    target[size - plane + 1] = size - 1
    return lax.ppermute(x, axis, sorted(target.items()))


def to_last(x, axis):
    size = lax.axis_size(axis)
    return lax.ppermute(x, axis, [(size - plane, size - 1)])


def split(x):
    high = x.astype(jnp.bfloat16)
    low = (x - high.astype(jnp.float32)).astype(jnp.bfloat16)
    return high, low


def halves(pair):
    real, imag = split(pair[0]), split(pair[1])
    return (real[0], imag[0]), (real[1], imag[1])


def dot(left, right, turned):
    dims = (((1,), (1 if turned else 0,)), ((), ()))
    return lax.dot_general(left, right, dims, preferred_element_type=jnp.float32)


def product(left, right, turned=False):
    (lrh, lih), (lrl, lil) = left
    (rrh, rih), (rrl, ril) = right
    rows = lrh.shape[0]
    high = jnp.concatenate([lrh, lih], axis=0)
    low = jnp.concatenate([lrl, lil], axis=0)
    by_real = dot(high, rrh, turned) + (dot(high, rrl, turned) + dot(low, rrh, turned))
    by_imag = dot(high, rih, turned) + (dot(high, ril, turned) + dot(low, rih, turned))
    return by_real[:rows] - by_imag[rows:], by_imag[:rows] + by_real[rows:]


def columns_product(left, right):
    high, low = right
    width = high.shape[1] // 2

    def real(k):
        by_high = dot(left[0][k], high, False) + dot(left[1][k], high, False)
        return by_high + dot(left[0][k], low, False)

    by_real, by_imag = real(0), real(1)
    return by_real[:, :width] - by_imag[:, width:], by_real[:, width:] + by_imag[:, :width]


def call(kernel, outs, scratch, flops, *args, aliases={}, places=None, out_places=None):
    shapes = outs if isinstance(outs, list) else [outs]
    moved = sum(a.size * a.dtype.itemsize for a in args)
    moved += sum(s.size * s.dtype.itemsize for s in shapes)
    in_specs = [pl.BlockSpec(memory_space=p) for p in places or (pltpu.VMEM,) * len(args)]
    out_specs = [pl.BlockSpec(memory_space=p) for p in out_places or (pltpu.VMEM,) * len(shapes)]
    return pl.pallas_call(
        kernel,
        out_shape=outs,
        in_specs=in_specs,
        out_specs=out_specs if isinstance(outs, list) else out_specs[0],
        scratch_shapes=scratch,
        input_output_aliases=aliases,
        compiler_params=pltpu.CompilerParams(vmem_limit_bytes=24 * 1024 * 1024),
        cost_estimate=pl.CostEstimate(flops=flops, bytes_accessed=moved, transcendentals=0),
    )(*args)


def f32(*shape):
    return jax.ShapeDtypeStruct(shape, jnp.float32)


def index_grid(size):
    row = lax.broadcasted_iota(jnp.int32, (size, size), 0)
    col = lax.broadcasted_iota(jnp.int32, (size, size), 1)
    return row, col


def pack_kernel(drawn_ref, packed_ref):
    first, second = drawn_ref[0, 0], drawn_ref[0, 1]
    row, col = index_grid(first.shape[0])
    mirrored = jnp.where(row >= col, first, -second).T
    packed_ref[...] = (jnp.where(row <= col, first, second) + mirrored) * 0.5


def unpacked(packed):
    row, col = index_grid(packed.shape[0])
    mirrored = packed.T
    real = jnp.where(row <= col, packed, mirrored)
    imag = jnp.where(row > col, packed, jnp.where(row < col, -mirrored, 0.0))
    return real, imag


def thirds(pair):
    return split(pair[0]), split(pair[1]), split(pair[0] + pair[1])


def three_products(left, right):
    def real(l, r):
        return dot(l[0], r[0], False) + (dot(l[0], r[1], False) + dot(l[1], r[0], False))

    ac, bd = real(left[0], right[0]), real(left[1], right[1])
    return ac - bd, real(left[2], right[2]) - (ac + bd)


def prepare_kernel(packed_ref, parts_ref, high_ref, low_ref):
    pair = unpacked(packed_ref[...])
    store(parts_ref, pair)
    for k, (high, low) in enumerate(thirds(pair)):
        high_ref[k] = high
        low_ref[k] = low


def magnus(parts_ref, high_ref, low_ref, packed, factor_ref):
    first = parts_ref[0], parts_ref[1]
    second = unpacked(packed)
    row, col = index_grid(packed.shape[0])
    identity = jnp.where(row == col, 1.0, 0.0).astype(jnp.float32)
    prepared = [(high_ref[k], low_ref[k]) for k in range(3)]
    both = three_products(thirds(second), prepared)
    comm_real = both[0] - both[0].T
    comm_imag = both[1] + both[1].T
    shrink = time_step * time_step / 12.0
    real = shrink * comm_real - 0.5 * time_step * (first[1] + second[1])
    imag = -0.5 * time_step * (first[0] + second[0]) - shrink * comm_imag
    exponent = thirds((real, imag))
    nested = (identity + real * 0.25, imag * 0.25)
    for order in (3.0, 2.0, 1.0):
        grown = three_products(thirds(nested), exponent)
        nested = (identity + grown[0] * (1.0 / order), grown[1] * (1.0 / order))
    factor_ref[0] = nested[0]
    factor_ref[1] = nested[1]


def factor_kernel(axis, parts_ref, high_ref, low_ref, pair_ref, next_ref, factor_ref):
    odd = lax.axis_index(axis) & 1
    magnus(parts_ref, high_ref, low_ref, jnp.where(odd == 0, pair_ref[...], next_ref[...]), factor_ref)


def late_kernel(axis, parts_ref, high_ref, low_ref, next_ref, factor_ref):
    me = lax.axis_index(axis)

    @pl.when(me == lax.axis_size(axis) - 1)
    def _():
        magnus(parts_ref, high_ref, low_ref, next_ref[...], factor_ref)


def load(ref, rows=slice(None)):
    return ref[0, rows, :], ref[1, rows, :]


def store(ref, pair, rows=slice(None)):
    ref[0, rows, :] = pair[0]
    ref[1, rows, :] = pair[1]


def chip_kernel(axis, own_ref, other_ref, half_ref, real_ref, imag_ref):
    odd = lax.axis_index(axis) & 1
    rows = half_ref.shape[1]
    half = pl.ds(pl.multiple_of(odd * rows, rows), rows)

    def put(left, right):
        pair = three_products(thirds(left), thirds(right))
        store(half_ref, pair)
        real_ref[...] = pair[0]
        imag_ref[...] = pair[1]

    @pl.when(odd == 0)
    def _():
        put(load(own_ref, half), load(other_ref))

    @pl.when(odd == 1)
    def _():
        put(load(other_ref, half), load(own_ref))


def get(high_ref, low_ref, q, rows=slice(None)):
    return (
        (high_ref[q, 0, rows, :], high_ref[q, 1, rows, :]),
        (low_ref[q, 0, rows, :], low_ref[q, 1, rows, :]),
    )


def get_pair(high_ref, low_ref, rows=slice(None)):
    return (
        (high_ref[0, rows, :], high_ref[1, rows, :]),
        (low_ref[0, rows, :], low_ref[1, rows, :]),
    )


def hold(axis, rel, other, k, piece, high_ref, low_ref):
    me = lax.axis_index(axis)
    rows = piece.shape[0]
    begin = pl.multiple_of(((me & 1) ^ other) * rows, rows)
    high, low = split(piece)
    high_ref[((me >> 1) & 3) ^ rel, k, pl.ds(begin, rows), :] = high
    low_ref[((me >> 1) & 3) ^ rel, k, pl.ds(begin, rows), :] = low


def near_kernel(axis, *refs):
    own, rest, (high_ref, low_ref, row_high_ref, row_low_ref) = refs[:2], refs[2:10], refs[10:]
    for k in range(2):
        for other in range(2):
            hold(axis, 0, other, k, own[other][k], high_ref, low_ref)
            hold(axis, 1, other, k, rest[2 * k + other][...], high_ref, low_ref)
            hold(axis, 2, other, k, rest[4 + 2 * k + other][...], high_ref, low_ref)
    begin = (lax.axis_index(axis) >> 1) & 2
    grown = product(get(high_ref, low_ref, begin), get(high_ref, low_ref, begin + 1))
    for k in range(2):
        row_high_ref[k], row_low_ref[k] = split(grown[k])


def core_rows(me, count):
    return pl.ds(pl.multiple_of((me & 1) * count, count), count)


def own_rows(me, count):
    return pl.ds(pl.multiple_of((me & (parts - 1)) * count, count), count)


def own_turned(me, count, columns, room_ref):
    begin = (me & (parts - 1)) * count
    width = room_ref.shape[0]
    block = pl.ds(pl.multiple_of(begin // width * width, width), width)
    inside = pl.ds(pl.multiple_of(begin % width, count), count)
    out = []
    for k in range(2):
        room_ref[...] = columns(k, block).T
        out.append(room_ref[inside, :])
    return out


def total_kernel(axis, level, *refs):
    pieces, (row_high_ref, row_low_ref) = refs[:4], refs[6:8]
    slice_ref, high_ref, low_ref, room_ref = refs[8:]
    for k in range(2):
        for other in range(2):
            hold(axis, 3, other, k, pieces[2 * k + other][...], high_ref, low_ref)
    me = lax.axis_index(axis)
    rows = own_rows(me, slice_ref.shape[1])
    upper, second_row = (me // level) & 1, (me >> 2) & 1
    row = get_pair(row_high_ref, row_low_ref)

    @pl.when((upper == 0) & (second_row == 0))
    def _():
        value = product(get_pair(row_high_ref, row_low_ref, rows), get(high_ref, low_ref, 2))
        store(slice_ref, product(halves(value), get(high_ref, low_ref, 3)))

    @pl.when((upper == 0) & (second_row == 1))
    def _():
        value = product(get(high_ref, low_ref, 0, rows), get(high_ref, low_ref, 1))
        store(slice_ref, product(halves(value), row))

    begin = (me & (parts - 1)) * slice_ref.shape[1]
    width = room_ref.shape[0]
    block = pl.ds(pl.multiple_of(begin // width * width, width), width)

    def columns(high, low):
        return (
            jnp.concatenate([high[0], high[1]], axis=1),
            jnp.concatenate([low[0], low[1]], axis=1),
        )

    def put(first, second, right):
        grown = columns_product(first, right)
        grown = columns_product(second, columns(*zip(split(grown[0]), split(grown[1]))))
        inside = pl.ds(pl.multiple_of(begin % width, slice_ref.shape[1]), slice_ref.shape[1])
        for k in range(2):
            room_ref[...] = grown[k].T
            slice_ref[k] = room_ref[inside, :]

    @pl.when((upper == 1) & (second_row == 1))
    def _():
        right = columns(
            [row_high_ref[k, :, block] for k in range(2)], [row_low_ref[k, :, block] for k in range(2)]
        )
        put(get(high_ref, low_ref, 1), get(high_ref, low_ref, 0), right)

    @pl.when((upper == 1) & (second_row == 0))
    def _():
        right = columns(
            [high_ref[3, k, :, block] for k in range(2)], [low_ref[3, k, :, block] for k in range(2)]
        )
        put(get(high_ref, low_ref, 2), row, right)


def prefix_kernel(axis, high_ref, low_ref, own_ref, other_ref, total_ref, local_ref, half_ref):
    me = lax.axis_index(axis)
    odd, chip = me & 1, (me >> 1) & 3
    last = me == lax.axis_size(axis) - 1
    first = get(high_ref, low_ref, 0)

    @pl.when((chip == 0) & (odd == 1))
    def _():
        for k in range(2):
            local_ref[k] = first[0][k].astype(jnp.float32) + first[1][k].astype(jnp.float32)

    @pl.when((chip == 0) & (odd == 0))
    def _():
        store(local_ref, load(own_ref))

    value = first
    for q in (1, 2, 3):

        @pl.when((chip == q) & (odd == 0))
        def _(value=value):
            store(local_ref, product(value, halves(load(own_ref))))

        if q == 3:

            @pl.when(last)
            def _(value=value):
                store(local_ref, product(value, halves(load(other_ref))))

        grown = product(value, get(high_ref, low_ref, q))
        store(total_ref, grown)
        value = halves(load(total_ref))

        @pl.when((chip == q) & (odd == 1) & jnp.logical_not(last))
        def _():
            store(local_ref, load(total_ref))

    store(half_ref, load(total_ref, core_rows(me, half_ref.shape[1])))


def cut_kernel(axis, level, total_ref, slice_ref, half_ref, room_ref):
    me = lax.axis_index(axis)
    count = slice_ref.shape[1]
    upper = (me // level) & 1
    store(half_ref, load(total_ref, core_rows(me, half_ref.shape[1])))

    @pl.when(upper == 0)
    def _():
        store(slice_ref, load(total_ref, own_rows(me, count)))

    @pl.when(upper == 1)
    def _():
        store(slice_ref, own_turned(me, count, lambda k, c: total_ref[k, :, c], room_ref))


def double_kernel(axis, level, total_ref, local_ref, mine_ref, other_ref, next_total_ref, next_local_ref):
    me = lax.axis_index(axis)
    odd, upper = me & 1, (me // level) & 1
    top = [jnp.where(odd == 0, mine_ref[k], other_ref[k]) for k in range(2)]
    low = [jnp.where(odd == 0, other_ref[k], mine_ref[k]) for k in range(2)]
    came = halves([jnp.concatenate([top[k], low[k]], axis=0) for k in range(2)])
    total = halves(load(total_ref))

    @pl.when(upper == 0)
    def _():
        store(next_total_ref, product(total, came))
        store(next_local_ref, load(local_ref))

    @pl.when(upper == 1)
    def _():
        store(next_total_ref, product(came, total))
        store(next_local_ref, product(came, halves(load(local_ref))))


def step_kernel(axis, level, came_ref, total_ref, slice_ref):
    block = (lax.axis_index(axis) // level) & 3

    @pl.when(block == 0)
    def _():
        store(slice_ref, product(halves(load(came_ref)), halves(load(total_ref)), True))

    @pl.when(block == 1)
    def _():
        store(slice_ref, product(halves(load(came_ref)), halves(load(total_ref))))

    @pl.when(block >= 2)
    def _():
        slice_ref[...] = came_ref[...]


def join_kernel(*refs):
    for place, ref in enumerate(refs[:4]):
        refs[4][place] = ref[...]


def local_kernel(axis, level, mine_ref, twin_ref, local_ref, late_ref, out_ref, high_ref, low_ref, whole_ref, sent):
    me = lax.axis_index(axis)
    half, size = mine_ref.shape[1], local_ref.shape[-1]
    upper = (me // level) & 1
    block = (me // level) & 3
    last = me == lax.axis_size(axis) - 1

    def give(pair):
        for k, (high, low) in enumerate(thirds(pair)):
            high_ref[k] = high
            low_ref[k] = low

    def finish(pair):
        store(whole_ref, [part.T for part in pair])
        copy = pltpu.make_async_copy(whole_ref, out_ref.at[0], sent)
        copy.start()
        copy.wait()

    @pl.when(block == 0)
    def _():
        finish(load(local_ref))

    @pl.when(block == 2)
    def _():
        order = [own_rows(me ^ mask, size // parts) for mask in (0, 2, 4, 6, 1, 3, 5, 7)]
        give([jnp.concatenate([local_ref[k, rows, :] for rows in order], axis=0).T for k in range(2)])

    @pl.when(upper == 1)
    def _():
        store(whole_ref, load(mine_ref), core_rows(me, half))
        store(whole_ref, load(twin_ref), core_rows(me ^ 1, half))
        grown = three_products(thirds(load(whole_ref)), thirds(load(local_ref)))

        @pl.when(block == 1)
        def _():
            finish(grown)

        @pl.when((block == 3) & jnp.logical_not(last))
        def _():
            give(grown)

        @pl.when(last)
        def _():
            give(three_products(thirds(grown), thirds(load(late_ref))))


def joined_pair(ref):
    return [ref[:, k].reshape(-1, ref.shape[-1]) for k in range(2)]


def early_kernel(axis, level, mine_ref, high_ref, low_ref, part_ref):
    block = (lax.axis_index(axis) // level) & 3
    half = part_ref.shape[1] // 2

    @pl.when(block == 2)
    def _():
        left = [(high_ref[k, :, :half], low_ref[k, :, :half]) for k in range(3)]
        store(part_ref, three_products(left, thirds(joined_pair(mine_ref))))

    @pl.when(block == 3)
    def _():
        right = [(high_ref[k], low_ref[k]) for k in range(3)]
        store(part_ref, three_products(thirds(joined_pair(mine_ref)), right), pl.ds(0, half))


def final_kernel(axis, level, part_ref, twin_ref, high_ref, low_ref, done_ref, out_ref, whole_ref, result_ref, sent):
    me = lax.axis_index(axis)
    block = (me // level) & 3
    size = whole_ref.shape[1]
    half = size // 2
    spans = [pl.ds(0, half), pl.ds(half, half)]

    def send(step):
        copy = pltpu.make_async_copy(result_ref.at[:, spans[step]], out_ref.at[0, :, spans[step]], sent.at[step])
        copy.start()
        return copy

    @pl.when(block == 2)
    def _():
        right = thirds(joined_pair(twin_ref))
        copies = []
        for step, rows in enumerate(spans):
            left = [(high_ref[k, rows, half:], low_ref[k, rows, half:]) for k in range(3)]
            grown = three_products(left, right)
            store(result_ref, [part_ref[k, rows, :] + grown[k] for k in range(2)], rows)
            copies.append(send(step))
        for copy in copies:
            copy.wait()

    @pl.when(block == 3)
    def _():
        right = [(high_ref[k], low_ref[k]) for k in range(3)]
        grown = three_products(thirds(joined_pair(twin_ref)), right)
        count = size // parts
        for place in range(4):
            rows = slice(place * count, (place + 1) * count)
            store(whole_ref, load(part_ref, rows), own_rows(me ^ (2 * place), count))
            store(whole_ref, [part[rows] for part in grown], own_rows(me ^ (2 * place + 1), count))
        copies = []
        for step, columns in enumerate(spans):
            store(result_ref, [whole_ref[k, :, columns].T for k in range(2)], columns)
            copies.append(send(step))
        for copy in copies:
            copy.wait()


def plane_slices(mine, axis, level):
    even = [mine] + [upper_exchanged(mine, axis, level, mask) for mask in (2, 4, 6)]
    shape = jax.ShapeDtypeStruct((4,) + mine.shape, mine.dtype)
    joined = call(join_kernel, shape, [], mine.size, *even)
    return joined, exchanged(joined, axis, 1)


def cumulative(samples):
    axis = "tm"
    devices = lax.axis_size(axis)
    size = samples.shape[-1]
    cube = 8 * size**3
    part = size // parts
    whole = f32(2, size, size)
    strip = f32(2, part, size)

    packed = call(pack_kernel, f32(size, size), [], size * size, samples)
    near_next = from_next(packed, axis)
    even_next = exchanged(packed, axis, 1)
    last_next = to_last(near_next, axis)
    third_shape = jax.ShapeDtypeStruct((3, size, size), jnp.bfloat16)
    prepared = call(prepare_kernel, [whole, third_shape, third_shape], [], size * size, packed)
    factor = call(functools.partial(factor_kernel, axis), whole, [], 9 * cube, *prepared, even_next, near_next)
    other = exchanged(factor, axis, 1)
    quarter = f32(size // 2, size)
    half, real, imag = call(
        functools.partial(chip_kernel, axis),
        [f32(2, size // 2, size), quarter, quarter],
        [],
        3 * cube // 2,
        factor,
        other,
    )

    y_real = exchanged(real, axis, 4)
    x_imag = exchanged(imag, axis, 2)
    y_imag = exchanged(imag, axis, 4)
    x_real = exchanged(real, axis, 2)
    far_real = exchanged(y_real, axis, 2)
    far_imag = exchanged(x_imag, axis, 4)
    both = [half, exchanged(half, axis, 1)]
    for piece in (x_real, x_imag, y_real, y_imag):
        both += [piece, exchanged(piece, axis, 1)]
    far = []
    for piece in (far_real, far_imag):
        far += [piece, exchanged(piece, axis, 1)]

    level = plane
    split_shape = jax.ShapeDtypeStruct((4, 2, size, size), jnp.bfloat16)
    row_shape = jax.ShapeDtypeStruct((2, size, size), jnp.bfloat16)
    high, low, row_high, row_low = call(
        functools.partial(near_kernel, axis), [split_shape, split_shape, row_shape, row_shape], [], 3 * cube, *both
    )
    turning = [pltpu.VMEM((128, size), jnp.float32)]
    mine, high, low = call(
        functools.partial(total_kernel, axis, level),
        [strip, split_shape, split_shape],
        turning,
        cube,
        *far,
        high,
        low,
        row_high,
        row_low,
        aliases={4: 1, 5: 2},
    )
    half_shape = f32(2, size // 2, size)
    total, local, bulk = call(
        functools.partial(prefix_kernel, axis), [whole, whole, half_shape], [], 12 * cube, high, low, factor, other
    )
    if devices > 4 * plane:
        while 4 * level < devices:
            half_of = lax.dynamic_slice_in_dim(total, (lax.axis_index(axis) & 1) * (size // 2), size // 2, 1)
            came = exchanged(half_of, axis, level)
            paired = exchanged(came, axis, 1)
            total, local = call(
                functools.partial(double_kernel, axis, level), [whole, whole], [], 6 * cube, total, local, came, paired
            )
            level = 2 * level
        mine, bulk = call(functools.partial(cut_kernel, axis, level), [strip, half_shape], turning, cube, total)
    came = lower_exchanged(mine, axis, level)
    step = call(functools.partial(step_kernel, axis, level), strip, [], 3 * cube // parts, came, total)
    below = exchanged(step, axis, 2 * level)
    came_bulk = exchanged(bulk, axis, level)
    twin_bulk = exchanged(came_bulk, axis, 1)
    room = [pltpu.VMEM((2, size, size), jnp.float32)]
    late = call(functools.partial(late_kernel, axis), whole, [], cube, *prepared, last_next)
    out_shape = f32(1, 2, size, size)
    out, high, low = call(
        functools.partial(local_kernel, axis, level),
        [out_shape, third_shape, third_shape],
        room + [pltpu.SemaphoreType.DMA(())],
        3 * cube,
        came_bulk,
        twin_bulk,
        local,
        late,
        out_places=(pl.ANY, pltpu.VMEM, pltpu.VMEM),
    )
    joined, twin = plane_slices(below, axis, level)
    early = call(functools.partial(early_kernel, axis, level), whole, [], cube, joined, high, low)
    return call(
        functools.partial(final_kernel, axis, level),
        out_shape,
        room + room + [pltpu.SemaphoreType.DMA((2,))],
        2 * cube,
        early,
        twin,
        high,
        low,
        out,
        places=(pltpu.VMEM,) * 4 + (pl.ANY,),
        out_places=(pl.ANY,),
        aliases={4: 0},
    )


def solution(mesh):
    in_specs = (P("tm", None, None, None),)
    out_specs = P("tm", None, None, None)
    return jax.shard_map(cumulative, mesh=mesh, in_specs=in_specs, out_specs=out_specs, check_vma=False)
```

```python
import functools

import jax
import jax.numpy as jnp
from jax import lax
from jax.experimental import pallas as pl
from jax.experimental.pallas import tpu as pltpu
from jax.sharding import PartitionSpec as P


time_step = 0.25
plane = 8
parts = 8


def exchanged(x, axis, mask):
    size = lax.axis_size(axis)
    return lax.ppermute(x, axis, [(i, i ^ mask) for i in range(size)])


def lower_exchanged(x, axis, level):
    size = lax.axis_size(axis)
    return lax.ppermute(x, axis, [(i, i ^ (level if (i // level) & 2 == 0 else 1)) for i in range(size)])


def upper_exchanged(x, axis, level, mask):
    size = lax.axis_size(axis)
    return lax.ppermute(x, axis, [(i, i ^ (mask if (i // level) & 2 else 1)) for i in range(size)])


def from_next(x, axis):
    size = lax.axis_size(axis)
    target = {i: i - 1 for i in range(1, size)}
    target[0] = size - plane
    target[size - plane + 1] = size - 1
    return lax.ppermute(x, axis, sorted(target.items()))


def to_last(x, axis):
    size = lax.axis_size(axis)
    return lax.ppermute(x, axis, [(size - plane, size - 1)])


def split(x):
    high = x.astype(jnp.bfloat16)
    low = (x - high.astype(jnp.float32)).astype(jnp.bfloat16)
    return high, low


def halves(pair):
    real, imag = split(pair[0]), split(pair[1])
    return (real[0], imag[0]), (real[1], imag[1])


def dot(left, right, turned):
    dims = (((1,), (1 if turned else 0,)), ((), ()))
    return lax.dot_general(left, right, dims, preferred_element_type=jnp.float32)


def product(left, right, turned=False):
    (lrh, lih), (lrl, lil) = left
    (rrh, rih), (rrl, ril) = right
    rows = lrh.shape[0]
    high = jnp.concatenate([lrh, lih], axis=0)
    low = jnp.concatenate([lrl, lil], axis=0)
    by_real = dot(high, rrh, turned) + (dot(high, rrl, turned) + dot(low, rrh, turned))
    by_imag = dot(high, rih, turned) + (dot(high, ril, turned) + dot(low, rih, turned))
    return by_real[:rows] - by_imag[rows:], by_imag[:rows] + by_real[rows:]


def columns_product(left, right):
    high, low = right
    width = high.shape[1] // 2

    def real(k):
        by_high = dot(left[0][k], high, False) + dot(left[1][k], high, False)
        return by_high + dot(left[0][k], low, False)

    by_real, by_imag = real(0), real(1)
    return by_real[:, :width] - by_imag[:, width:], by_real[:, width:] + by_imag[:, :width]


def call(kernel, outs, scratch, flops, *args, aliases={}, places=None, out_places=None):
    shapes = outs if isinstance(outs, list) else [outs]
    moved = sum(a.size * a.dtype.itemsize for a in args)
    moved += sum(s.size * s.dtype.itemsize for s in shapes)
    in_specs = [pl.BlockSpec(memory_space=p) for p in places or (pltpu.VMEM,) * len(args)]
    out_specs = [pl.BlockSpec(memory_space=p) for p in out_places or (pltpu.VMEM,) * len(shapes)]
    return pl.pallas_call(
        kernel,
        out_shape=outs,
        in_specs=in_specs,
        out_specs=out_specs if isinstance(outs, list) else out_specs[0],
        scratch_shapes=scratch,
        input_output_aliases=aliases,
        compiler_params=pltpu.CompilerParams(vmem_limit_bytes=24 * 1024 * 1024),
        cost_estimate=pl.CostEstimate(flops=flops, bytes_accessed=moved, transcendentals=0),
    )(*args)


def f32(*shape):
    return jax.ShapeDtypeStruct(shape, jnp.float32)


def index_grid(size):
    row = lax.broadcasted_iota(jnp.int32, (size, size), 0)
    col = lax.broadcasted_iota(jnp.int32, (size, size), 1)
    return row, col


def pack_kernel(drawn_ref, packed_ref):
    first, second = drawn_ref[0, 0], drawn_ref[0, 1]
    row, col = index_grid(first.shape[0])
    mirrored = jnp.where(row >= col, first, -second).T
    packed_ref[...] = (jnp.where(row <= col, first, second) + mirrored) * 0.5


def unpacked(packed):
    row, col = index_grid(packed.shape[0])
    mirrored = packed.T
    real = jnp.where(row <= col, packed, mirrored)
    imag = jnp.where(row > col, packed, jnp.where(row < col, -mirrored, 0.0))
    return real, imag


def thirds(pair):
    return split(pair[0]), split(pair[1]), split(pair[0] + pair[1])


def three_products(left, right):
    def real(l, r):
        return dot(l[0], r[0], False) + (dot(l[0], r[1], False) + dot(l[1], r[0], False))

    ac, bd = real(left[0], right[0]), real(left[1], right[1])
    return ac - bd, real(left[2], right[2]) - (ac + bd)


def prepare_kernel(packed_ref, parts_ref, high_ref, low_ref):
    pair = unpacked(packed_ref[...])
    store(parts_ref, pair)
    for k, (high, low) in enumerate(thirds(pair)):
        high_ref[k] = high
        low_ref[k] = low


def magnus(parts_ref, high_ref, low_ref, packed, factor_ref):
    first = parts_ref[0], parts_ref[1]
    second = unpacked(packed)
    row, col = index_grid(packed.shape[0])
    identity = jnp.where(row == col, 1.0, 0.0).astype(jnp.float32)
    prepared = [(high_ref[k], low_ref[k]) for k in range(3)]
    both = three_products(thirds(second), prepared)
    comm_real = both[0] - both[0].T
    comm_imag = both[1] + both[1].T
    shrink = time_step * time_step / 12.0
    real = shrink * comm_real - 0.5 * time_step * (first[1] + second[1])
    imag = -0.5 * time_step * (first[0] + second[0]) - shrink * comm_imag
    exponent = thirds((real, imag))
    nested = (identity + real * 0.25, imag * 0.25)
    for order in (3.0, 2.0, 1.0):
        grown = three_products(thirds(nested), exponent)
        nested = (identity + grown[0] * (1.0 / order), grown[1] * (1.0 / order))
    factor_ref[0] = nested[0]
    factor_ref[1] = nested[1]


def factor_kernel(axis, parts_ref, high_ref, low_ref, pair_ref, next_ref, factor_ref):
    odd = lax.axis_index(axis) & 1
    magnus(parts_ref, high_ref, low_ref, jnp.where(odd == 0, pair_ref[...], next_ref[...]), factor_ref)


def late_kernel(axis, parts_ref, high_ref, low_ref, next_ref, factor_ref):
    me = lax.axis_index(axis)

    @pl.when(me == lax.axis_size(axis) - 1)
    def _():
        magnus(parts_ref, high_ref, low_ref, next_ref[...], factor_ref)


def load(ref, rows=slice(None)):
    return ref[0, rows, :], ref[1, rows, :]


def store(ref, pair, rows=slice(None)):
    ref[0, rows, :] = pair[0]
    ref[1, rows, :] = pair[1]


def chip_kernel(axis, own_ref, other_ref, half_ref, real_ref, imag_ref):
    odd = lax.axis_index(axis) & 1
    rows = half_ref.shape[1]
    half = pl.ds(pl.multiple_of(odd * rows, rows), rows)

    def put(left, right):
        pair = three_products(thirds(left), thirds(right))
        store(half_ref, pair)
        real_ref[...] = pair[0]
        imag_ref[...] = pair[1]

    @pl.when(odd == 0)
    def _():
        put(load(own_ref, half), load(other_ref))

    @pl.when(odd == 1)
    def _():
        put(load(other_ref, half), load(own_ref))


def get(high_ref, low_ref, q, rows=slice(None)):
    return (
        (high_ref[q, 0, rows, :], high_ref[q, 1, rows, :]),
        (low_ref[q, 0, rows, :], low_ref[q, 1, rows, :]),
    )


def get_pair(high_ref, low_ref, rows=slice(None)):
    return (
        (high_ref[0, rows, :], high_ref[1, rows, :]),
        (low_ref[0, rows, :], low_ref[1, rows, :]),
    )


def hold(axis, rel, other, k, piece, high_ref, low_ref):
    me = lax.axis_index(axis)
    rows = piece.shape[0]
    begin = pl.multiple_of(((me & 1) ^ other) * rows, rows)
    high, low = split(piece)
    high_ref[((me >> 1) & 3) ^ rel, k, pl.ds(begin, rows), :] = high
    low_ref[((me >> 1) & 3) ^ rel, k, pl.ds(begin, rows), :] = low


def near_kernel(axis, *refs):
    own, rest, (high_ref, low_ref, row_high_ref, row_low_ref) = refs[:2], refs[2:10], refs[10:]
    for k in range(2):
        for other in range(2):
            hold(axis, 0, other, k, own[other][k], high_ref, low_ref)
            hold(axis, 1, other, k, rest[2 * k + other][...], high_ref, low_ref)
            hold(axis, 2, other, k, rest[4 + 2 * k + other][...], high_ref, low_ref)
    begin = (lax.axis_index(axis) >> 1) & 2
    grown = product(get(high_ref, low_ref, begin), get(high_ref, low_ref, begin + 1))
    for k in range(2):
        row_high_ref[k], row_low_ref[k] = split(grown[k])


def core_rows(me, count):
    return pl.ds(pl.multiple_of((me & 1) * count, count), count)


def own_rows(me, count):
    return pl.ds(pl.multiple_of((me & (parts - 1)) * count, count), count)


def own_turned(me, count, columns, room_ref):
    begin = (me & (parts - 1)) * count
    width = room_ref.shape[0]
    block = pl.ds(pl.multiple_of(begin // width * width, width), width)
    inside = pl.ds(pl.multiple_of(begin % width, count), count)
    out = []
    for k in range(2):
        room_ref[...] = columns(k, block).T
        out.append(room_ref[inside, :])
    return out


def total_kernel(axis, level, *refs):
    pieces, (row_high_ref, row_low_ref) = refs[:4], refs[6:8]
    slice_ref, high_ref, low_ref, room_ref = refs[8:]
    for k in range(2):
        for other in range(2):
            hold(axis, 3, other, k, pieces[2 * k + other][...], high_ref, low_ref)
    me = lax.axis_index(axis)
    rows = own_rows(me, slice_ref.shape[1])
    block, second_row = (me // level) & 3, (me >> 2) & 1
    row = get_pair(row_high_ref, row_low_ref)

    @pl.when((block == 0) & (second_row == 0))
    def _():
        value = product(get_pair(row_high_ref, row_low_ref, rows), get(high_ref, low_ref, 2))
        store(slice_ref, product(halves(value), get(high_ref, low_ref, 3)))

    @pl.when((block == 0) & (second_row == 1))
    def _():
        value = product(get(high_ref, low_ref, 0, rows), get(high_ref, low_ref, 1))
        store(slice_ref, product(halves(value), row))

    begin = (me & (parts - 1)) * slice_ref.shape[1]
    width = room_ref.shape[0]
    columns_of = pl.ds(pl.multiple_of(begin // width * width, width), width)

    def columns(high, low):
        return (
            jnp.concatenate([high[0], high[1]], axis=1),
            jnp.concatenate([low[0], low[1]], axis=1),
        )

    def put(first, second, right):
        grown = columns_product(first, right)
        grown = columns_product(second, columns(*zip(split(grown[0]), split(grown[1]))))
        inside = pl.ds(pl.multiple_of(begin % width, slice_ref.shape[1]), slice_ref.shape[1])
        for k in range(2):
            room_ref[...] = grown[k].T
            slice_ref[k] = room_ref[inside, :]

    @pl.when((block == 1) & (second_row == 1))
    def _():
        right = columns(
            [row_high_ref[k, :, columns_of] for k in range(2)], [row_low_ref[k, :, columns_of] for k in range(2)]
        )
        put(get(high_ref, low_ref, 1), get(high_ref, low_ref, 0), right)

    @pl.when((block == 1) & (second_row == 0))
    def _():
        right = columns(
            [high_ref[3, k, :, columns_of] for k in range(2)], [low_ref[3, k, :, columns_of] for k in range(2)]
        )
        put(get(high_ref, low_ref, 2), row, right)

    @pl.when(block >= 2)
    def _():
        slice_ref[...] = jnp.zeros_like(slice_ref)


def prefix_kernel(axis, high_ref, low_ref, own_ref, other_ref, total_ref, local_ref, half_ref):
    me = lax.axis_index(axis)
    odd, chip = me & 1, (me >> 1) & 3
    last = me == lax.axis_size(axis) - 1
    first = get(high_ref, low_ref, 0)

    @pl.when((chip == 0) & (odd == 1))
    def _():
        for k in range(2):
            local_ref[k] = first[0][k].astype(jnp.float32) + first[1][k].astype(jnp.float32)

    @pl.when((chip == 0) & (odd == 0))
    def _():
        store(local_ref, load(own_ref))

    value = first
    for q in (1, 2, 3):

        @pl.when((chip == q) & (odd == 0))
        def _(value=value):
            store(local_ref, product(value, halves(load(own_ref))))

        if q == 3:

            @pl.when(last)
            def _(value=value):
                store(local_ref, product(value, halves(load(other_ref))))

        grown = product(value, get(high_ref, low_ref, q))
        store(total_ref, grown)
        value = halves(load(total_ref))

        @pl.when((chip == q) & (odd == 1) & jnp.logical_not(last))
        def _():
            store(local_ref, load(total_ref))

    store(half_ref, load(total_ref, core_rows(me, half_ref.shape[1])))


def cut_kernel(axis, level, total_ref, slice_ref, half_ref, room_ref):
    me = lax.axis_index(axis)
    count = slice_ref.shape[1]
    upper = (me // level) & 1
    store(half_ref, load(total_ref, core_rows(me, half_ref.shape[1])))

    @pl.when(upper == 0)
    def _():
        store(slice_ref, load(total_ref, own_rows(me, count)))

    @pl.when(upper == 1)
    def _():
        store(slice_ref, own_turned(me, count, lambda k, c: total_ref[k, :, c], room_ref))


def double_kernel(axis, level, total_ref, local_ref, mine_ref, other_ref, next_total_ref, next_local_ref):
    me = lax.axis_index(axis)
    odd, upper = me & 1, (me // level) & 1
    top = [jnp.where(odd == 0, mine_ref[k], other_ref[k]) for k in range(2)]
    low = [jnp.where(odd == 0, other_ref[k], mine_ref[k]) for k in range(2)]
    came = halves([jnp.concatenate([top[k], low[k]], axis=0) for k in range(2)])
    total = halves(load(total_ref))

    @pl.when(upper == 0)
    def _():
        store(next_total_ref, product(total, came))
        store(next_local_ref, load(local_ref))

    @pl.when(upper == 1)
    def _():
        store(next_total_ref, product(came, total))
        store(next_local_ref, product(came, halves(load(local_ref))))


def step_kernel(axis, level, came_ref, total_ref, slice_ref):
    block = (lax.axis_index(axis) // level) & 3

    @pl.when(block == 0)
    def _():
        store(slice_ref, product(halves(load(came_ref)), halves(load(total_ref)), True))

    @pl.when(block == 1)
    def _():
        store(slice_ref, product(halves(load(came_ref)), halves(load(total_ref))))

    @pl.when(block >= 2)
    def _():
        slice_ref[...] = came_ref[...]


def join_kernel(*refs):
    for place, ref in enumerate(refs[:4]):
        refs[4][place] = ref[...]


def local_kernel(axis, level, mine_ref, twin_ref, local_ref, late_ref, out_ref, high_ref, low_ref, whole_ref, sent):
    me = lax.axis_index(axis)
    half, size = mine_ref.shape[1], local_ref.shape[-1]
    upper = (me // level) & 1
    block = (me // level) & 3
    last = me == lax.axis_size(axis) - 1

    def give(pair):
        for k, (high, low) in enumerate(thirds(pair)):
            high_ref[k] = high
            low_ref[k] = low

    def finish(pair):
        store(whole_ref, [part.T for part in pair])
        copy = pltpu.make_async_copy(whole_ref, out_ref.at[0], sent)
        copy.start()
        copy.wait()

    @pl.when(block == 0)
    def _():
        finish(load(local_ref))

    @pl.when(block == 2)
    def _():
        order = [own_rows(me ^ mask, size // parts) for mask in (0, 2, 4, 6, 1, 3, 5, 7)]
        give([jnp.concatenate([local_ref[k, rows, :] for rows in order], axis=0).T for k in range(2)])

    @pl.when(upper == 1)
    def _():
        store(whole_ref, load(mine_ref), core_rows(me, half))
        store(whole_ref, load(twin_ref), core_rows(me ^ 1, half))
        grown = three_products(thirds(load(whole_ref)), thirds(load(local_ref)))

        @pl.when(block == 1)
        def _():
            finish(grown)

        @pl.when((block == 3) & jnp.logical_not(last))
        def _():
            give(grown)

        @pl.when(last)
        def _():
            give(three_products(thirds(grown), thirds(load(late_ref))))


def joined_pair(ref):
    return [ref[:, k].reshape(-1, ref.shape[-1]) for k in range(2)]


def early_kernel(axis, level, mine_ref, high_ref, low_ref, part_ref):
    block = (lax.axis_index(axis) // level) & 3
    half = part_ref.shape[1] // 2

    @pl.when(block == 2)
    def _():
        left = [(high_ref[k, :, :half], low_ref[k, :, :half]) for k in range(3)]
        store(part_ref, three_products(left, thirds(joined_pair(mine_ref))))

    @pl.when(block == 3)
    def _():
        right = [(high_ref[k], low_ref[k]) for k in range(3)]
        store(part_ref, three_products(thirds(joined_pair(mine_ref)), right), pl.ds(0, half))


def final_kernel(axis, level, part_ref, twin_ref, high_ref, low_ref, done_ref, out_ref, whole_ref, result_ref, sent):
    me = lax.axis_index(axis)
    block = (me // level) & 3
    size = whole_ref.shape[1]
    half = size // 2
    spans = [pl.ds(0, half), pl.ds(half, half)]

    def send(step):
        copy = pltpu.make_async_copy(result_ref.at[:, spans[step]], out_ref.at[0, :, spans[step]], sent.at[step])
        copy.start()
        return copy

    @pl.when(block == 2)
    def _():
        right = thirds(joined_pair(twin_ref))
        copies = []
        for step, rows in enumerate(spans):
            left = [(high_ref[k, rows, half:], low_ref[k, rows, half:]) for k in range(3)]
            grown = three_products(left, right)
            store(result_ref, [part_ref[k, rows, :] + grown[k] for k in range(2)], rows)
            copies.append(send(step))
        for copy in copies:
            copy.wait()

    @pl.when(block == 3)
    def _():
        right = [(high_ref[k], low_ref[k]) for k in range(3)]
        grown = three_products(thirds(joined_pair(twin_ref)), right)
        count = size // parts
        for place in range(4):
            rows = slice(place * count, (place + 1) * count)
            store(whole_ref, load(part_ref, rows), own_rows(me ^ (2 * place), count))
            store(whole_ref, [part[rows] for part in grown], own_rows(me ^ (2 * place + 1), count))
        copies = []
        for step, columns in enumerate(spans):
            store(result_ref, [whole_ref[k, :, columns].T for k in range(2)], columns)
            copies.append(send(step))
        for copy in copies:
            copy.wait()


def plane_slices(mine, axis, level):
    even = [mine] + [upper_exchanged(mine, axis, level, mask) for mask in (2, 4, 6)]
    shape = jax.ShapeDtypeStruct((4,) + mine.shape, mine.dtype)
    joined = call(join_kernel, shape, [], mine.size, *even)
    return joined, exchanged(joined, axis, 1)


def cumulative(samples):
    axis = "tm"
    devices = lax.axis_size(axis)
    size = samples.shape[-1]
    cube = 8 * size**3
    part = size // parts
    whole = f32(2, size, size)
    strip = f32(2, part, size)

    packed = call(pack_kernel, f32(size, size), [], size * size, samples)
    near_next = from_next(packed, axis)
    even_next = exchanged(packed, axis, 1)
    last_next = to_last(near_next, axis)
    third_shape = jax.ShapeDtypeStruct((3, size, size), jnp.bfloat16)
    prepared = call(prepare_kernel, [whole, third_shape, third_shape], [], size * size, packed)
    factor = call(functools.partial(factor_kernel, axis), whole, [], 9 * cube, *prepared, even_next, near_next)
    other = exchanged(factor, axis, 1)
    quarter = f32(size // 2, size)
    half, real, imag = call(
        functools.partial(chip_kernel, axis),
        [f32(2, size // 2, size), quarter, quarter],
        [],
        3 * cube // 2,
        factor,
        other,
    )

    y_real = exchanged(real, axis, 4)
    x_imag = exchanged(imag, axis, 2)
    y_imag = exchanged(imag, axis, 4)
    x_real = exchanged(real, axis, 2)
    far_real = exchanged(y_real, axis, 2)
    far_imag = exchanged(x_imag, axis, 4)
    both = [half, exchanged(half, axis, 1)]
    for piece in (x_real, x_imag, y_real, y_imag):
        both += [piece, exchanged(piece, axis, 1)]
    far = []
    for piece in (far_real, far_imag):
        far += [piece, exchanged(piece, axis, 1)]

    level = plane
    split_shape = jax.ShapeDtypeStruct((4, 2, size, size), jnp.bfloat16)
    row_shape = jax.ShapeDtypeStruct((2, size, size), jnp.bfloat16)
    high, low, row_high, row_low = call(
        functools.partial(near_kernel, axis), [split_shape, split_shape, row_shape, row_shape], [], 3 * cube, *both
    )
    turning = [pltpu.VMEM((128, size), jnp.float32)]
    mine, high, low = call(
        functools.partial(total_kernel, axis, level),
        [strip, split_shape, split_shape],
        turning,
        cube,
        *far,
        high,
        low,
        row_high,
        row_low,
        aliases={4: 1, 5: 2},
    )
    half_shape = f32(2, size // 2, size)
    total, local, bulk = call(
        functools.partial(prefix_kernel, axis), [whole, whole, half_shape], [], 12 * cube, high, low, factor, other
    )
    if devices > 4 * plane:
        while 4 * level < devices:
            half_of = lax.dynamic_slice_in_dim(total, (lax.axis_index(axis) & 1) * (size // 2), size // 2, 1)
            came = exchanged(half_of, axis, level)
            paired = exchanged(came, axis, 1)
            total, local = call(
                functools.partial(double_kernel, axis, level), [whole, whole], [], 6 * cube, total, local, came, paired
            )
            level = 2 * level
        mine, bulk = call(functools.partial(cut_kernel, axis, level), [strip, half_shape], turning, cube, total)
    came = lower_exchanged(mine, axis, level)
    step = call(functools.partial(step_kernel, axis, level), strip, [], 3 * cube // parts, came, total)
    below = exchanged(step, axis, 2 * level)
    came_bulk = exchanged(bulk, axis, level)
    twin_bulk = exchanged(came_bulk, axis, 1)
    room = [pltpu.VMEM((2, size, size), jnp.float32)]
    late = call(functools.partial(late_kernel, axis), whole, [], cube, *prepared, last_next)
    out_shape = f32(1, 2, size, size)
    out, high, low = call(
        functools.partial(local_kernel, axis, level),
        [out_shape, third_shape, third_shape],
        room + [pltpu.SemaphoreType.DMA(())],
        3 * cube,
        came_bulk,
        twin_bulk,
        local,
        late,
        out_places=(pl.ANY, pltpu.VMEM, pltpu.VMEM),
    )
    joined, twin = plane_slices(below, axis, level)
    early = call(functools.partial(early_kernel, axis, level), whole, [], cube, joined, high, low)
    return call(
        functools.partial(final_kernel, axis, level),
        out_shape,
        room + room + [pltpu.SemaphoreType.DMA((2,))],
        2 * cube,
        early,
        twin,
        high,
        low,
        out,
        places=(pltpu.VMEM,) * 4 + (pl.ANY,),
        out_places=(pl.ANY,),
        aliases={4: 0},
    )


def solution(mesh):
    in_specs = (P("tm", None, None, None),)
    out_specs = P("tm", None, None, None)
    return jax.shard_map(cumulative, mesh=mesh, in_specs=in_specs, out_specs=out_specs, check_vma=False)
```
